256 devices in a mesh: rows: 64 (over x, z, core), grp: 4 (over y).
Axes of the slice: x: 4, y: 4, z: 8, core: 2. Of those that a mesh axis runs over, the one named last changes fastest.
Arguments:
- tile_factor: bfloat16 [512, 128, 128], P(('rows', 'grp')), may hold values from -6 to 6
- coupling: bfloat16 [512, 3, 128, 128], P(('rows', 'grp')), may hold values from -6 to 6
- nbr_list: int32 [512, 4], P('rows'), may hold values from 0 to 511, as said below
- setup_slot: int32 [64, 8], P('rows'), may hold values from 0 to 7, each once within a row
- residual: float32 [256, 65536], P('grp', 'rows'), may hold values from -6 to 6
Outputs:
- factor_rows: float32 [512, 128, 512], P(('rows', 'grp'))
- preconditioned: float32 [256, 65536], P('grp', 'rows')
The draws below stay inside these ranges and needn't reach their ends.
Inputs may be any that keep to these rules, and one draw needn't show every extreme that they name: `nbr_list`: row i lists 4 distinct block rows: i itself, at some position, and others at distance 1, 3 or 4 from i. `setup_slot`: each slab's row holds every slot once.
All inputs are finite; a program needn't handle non-finite values.
Results may differ from the reference program's by a relative error of at most 0.00065.
Values may be sent and summed in bfloat16 or wider, within the bound.
A program may use at most 64 MiB of HBM per device.

```python
import jax
import jax.numpy as jnp
from jax import lax

B = 128
PAT = 4
COUPLES = 3
NBR = 8
PLANE = 4
NCOL = 256
SLABS = 64
NB = 512
CELLS = 65536


def draw_nbr_list(key, part):
    key_one, key_two = jax.random.split(key)
    reach = jnp.array([1, PLANE - 1, PLANE], dtype=jnp.int32)
    offsets = jnp.concatenate([-reach, reach])
    row_ids = jnp.arange(NB, dtype=jnp.int32)[:, None]
    targets = row_ids + offsets[None, :]
    inside = (targets >= 0) & (targets < NB)
    span_count = 6
    scores = jax.random.randint(key_one, (NB, span_count), 0, 4096) * span_count + jnp.arange(span_count, dtype=jnp.int32)[None, :]
    scores = scores + jnp.where(inside, 1 << 24, 0)
    ranking = jnp.argsort(-scores, axis=1)
    picked = jnp.take_along_axis(targets, ranking[:, :PAT - 1], axis=1)
    entries = jnp.concatenate([picked, row_ids], axis=1)
    position_keys = jax.random.randint(key_two, (NB, PAT), 0, 4096) * PAT + jnp.arange(PAT, dtype=jnp.int32)[None, :]
    placing = jnp.argsort(position_keys, axis=1)
    return jnp.take_along_axis(entries, placing, axis=1).astype(jnp.int32)


def steps_of(stream_key, extent, shards, low, largest):
    level, own = 1.0, jax.random.fold_in(stream_key, 6)
    for position, blocks in shards:
        heights = jnp.exp(jax.random.uniform(jax.random.fold_in(own, position), (blocks,), jnp.float32, low / len(shards), largest / len(shards)))
        level = level * jnp.repeat(heights, extent[position] // blocks).reshape([-1 if axis == position else 1 for axis in range(len(extent))])
    return level


def gaussian(rng, shape, deviation, most, cuts=(), kind=jnp.bfloat16):
    values = jax.random.normal(rng, shape, jnp.float32) * deviation
    if len(cuts) > 0:
        values = steps_of(rng, shape, cuts, -0.22, 0.18) * values
    return jnp.clip(values, min=-most, max=most).astype(kind)


def setup_inputs(seed: int = 0) -> dict:
    splits = jax.random.split(jax.random.key(seed), 6)
    return {
        "tile_factor": gaussian(splits[0], (NB, B, B), 1.0, 6.0, ((0, 256),)),
        "coupling": gaussian(splits[1], (NB, COUPLES, B, B), 1.0, 6.0, ((0, 256),)),
        "nbr_list": draw_nbr_list(jax.random.fold_in(splits[5], 71), 0),
        "setup_slot": jax.vmap(lambda own: jax.random.permutation(own, NBR))(jax.random.split(splits[3], SLABS)).reshape((SLABS, NBR)).astype(jnp.int32),
        "residual": gaussian(splits[4], (NCOL, CELLS), 1.0, 6.0, ((0, 4), (1, 64)), jnp.float32),
    }


def form_diag(factors):
    tile_order = factors.shape[-1]
    square = jnp.einsum('nik,njk->nij', factors.astype(jnp.float32), factors.astype(jnp.float32), preferred_element_type=jnp.float32)
    return 2.0 * jnp.eye(tile_order, dtype=jnp.float32) + square / tile_order

def setup_rows(diag_tiles, coupling_tiles, pattern, select):
    count_rows = diag_tiles.shape[0]
    pieces = diag_tiles.shape[1]
    tile_order = diag_tiles.shape[2]
    offsets = [0, 1, PLANE]
    system = jnp.zeros((count_rows, pieces, tile_order, pieces, tile_order), jnp.float32)
    for first in range(len(offsets)):
        for second in range(len(offsets)):
            hit = (pattern[:, :, None] + offsets[first] == pattern[:, None, :] + offsets[second]).astype(jnp.float32)
            product = jnp.einsum('naik,nbjk->naibj', coupling_tiles[:, :, first].astype(jnp.float32), coupling_tiles[:, :, second].astype(jnp.float32), preferred_element_type=jnp.float32)
            system = system + product * hit[:, :, None, :, None]
    system = system / tile_order
    placed = diag_tiles[:, :, :, None, :] * jnp.eye(pieces, dtype=jnp.float32)[None, :, None, :, None]
    system = (system + placed).reshape(count_rows, pieces * tile_order, pieces * tile_order)
    selector = (select[:, :, None, None] * jnp.eye(tile_order, dtype=jnp.float32)[None, None]).reshape(count_rows, pieces * tile_order, tile_order)
    lower_factor = jnp.linalg.cholesky(system)
    half_solve = jax.scipy.linalg.solve_triangular(lower_factor, selector, lower=True)
    solved = jax.scipy.linalg.solve_triangular(lower_factor, half_solve, lower=True, trans=1)
    corner = jnp.sum(solved.reshape(count_rows, pieces, tile_order, tile_order) * select[:, :, None, None], axis=1)
    corner_factor = jnp.linalg.cholesky(corner)
    return jax.scipy.linalg.solve_triangular(corner_factor, jnp.swapaxes(solved, 1, 2), lower=True)

def reference(tile_factor, coupling, nbr_list, setup_slot, residual):
    diag_all = form_diag(tile_factor)
    columns = residual.shape[0]
    res_blocks = residual.reshape(columns, NB, B)

    def per_slab(running, slab_index):
        row_ids = slab_index * NBR + jnp.arange(NBR, dtype=jnp.int32)
        pattern = lax.dynamic_slice_in_dim(nbr_list, slab_index * NBR, NBR, 0)
        select = (pattern == row_ids[:, None]).astype(jnp.float32)
        factor = setup_rows(diag_all[pattern], coupling[pattern], pattern, select)
        picked = res_blocks[:, pattern].reshape(columns, NBR, PAT * B)
        reduced = jnp.einsum('nbq,cnq->cnb', factor, picked, precision=lax.Precision.HIGHEST)
        contributions = jnp.einsum('nbq,cnb->cnq', factor, reduced, precision=lax.Precision.HIGHEST)
        running = running.at[:, pattern.reshape(-1)].add(contributions.reshape(columns, NBR * PAT, B))
        return (running, factor)
    start = jnp.zeros((columns, NB, B), jnp.float32)
    result, factors = lax.scan(per_slab, start, jnp.arange(SLABS, dtype=jnp.int32))
    matches = setup_slot[:, :, None] == jnp.arange(NBR, dtype=jnp.int32)[None, None, :]
    inverse = jnp.sum(jnp.where(matches, jnp.arange(NBR, dtype=jnp.int32)[None, :, None], 0), axis=1).astype(jnp.int32)
    ordered = jnp.take_along_axis(factors, inverse[:, :, None, None], axis=1)
    return (ordered.reshape(NB, B, PAT * B), result.reshape(columns, NB * B))
```

```python
import functools

import jax
import jax.numpy as jnp
from jax import lax
from jax.experimental import pallas as pl
from jax.experimental.pallas import tpu as pltpu
from jax.sharding import PartitionSpec as P

B = 128
PAT = 4
NBR = 8
F32=jnp.float32; BF=jnp.bfloat16

def split(x):
    h = x.astype(BF)
    l = (x - h.astype(F32)).astype(BF)
    return h, l

def dg(a, b, ca, cb):
    return lax.dot_general(a, b, (((ca,), (cb,)), ((), ())), preferred_element_type=F32)

def mm(a, b, ca=1, cb=0):
    ah, al = a
    bh, bl = b
    return dg(ah, bh, ca, cb) + (dg(ah, bl, ca, cb) + dg(al, bh, ca, cb))

def eye(n=128):
    r = lax.broadcasted_iota(jnp.int32, (n, n), 0)
    c = lax.broadcasted_iota(jnp.int32, (n, n), 1)
    return (r == c).astype(F32)

def inverses(mats, K, newton):
    I = eye()
    alphas = []
    Rs, Ys = [], []
    for A in mats:
        norm = jnp.max(jnp.sum(jnp.abs(A), axis=0, keepdims=True), axis=1, keepdims=True)
        al = 1.98 / norm
        alphas.append(al)
        R = I - A * al
        Rs.append(R); Ys.append(I + R)
    for j in range(K):
        for m in range(len(mats)):
            r = split(Rs[m])
            y = split(Ys[m]) if j else None
            R2 = mm(r, r)
            r2 = split(R2)
            Ys[m] = Ys[m] + mm(split(Ys[m]), r2)
            Rs[m] = R2
    Xs = [y * a for y, a in zip(Ys, alphas)]
    for _ in range(newton):
        Es = [I - mm(split(A), split(X)) for A, X in zip(mats, Xs)]
        Xs = [X + mm(split(X), split(E)) for X, E in zip(Xs, Es)]
    return Xs

def uinv(mats):
    n = 128
    Ws = list(mats)
    col = lax.broadcasted_iota(jnp.int32, (1, n), 1)
    ds = [[] for _ in mats]
    slabs = [[W[8*t:8*t+8, :] for t in range(16)] for W in Ws]
    rowi = lax.broadcasted_iota(jnp.int32, (8, 1), 0)
    for k in range(n - 1, -1, -1):
        t, s = divmod(k, 8)
        for m in range(len(mats)):
            sl = slabs[m]
            piv_row = sl[t][s:s+1, :]
            d = piv_row[:, k:k+1]
            rinv = 1.0 / d
            prow = jnp.where(col == k, 1.0, piv_row * 1.0)
            pr = piv_row * rinv
            pr = jnp.where(col == k, 1.0 + rinv, pr)
            for tt in range(t + 1):
                c = sl[tt][:, k:k+1]
                if tt == t:
                    if s == 0:
                        continue
                    c = jnp.where(rowi < s, c, 0.0)
                sl[tt] = sl[tt] - c * pr
            fin = jnp.where(col < k, 0.0, jnp.where(col == k, 1.0, piv_row)) * lax.rsqrt(d)
            sl[t] = jnp.where(rowi == s, fin, sl[t])
    return [jnp.concatenate(sl, axis=0) for sl in slabs]

TX = {1: 1, 3: 2, 4: 2, -1: 0, -3: 1, -4: 0}

def edge(dl):
    def pick(d):
        return jnp.where(d == 1, 1, jnp.where((d == 3) | (d == 4), 2, jnp.where(d == -3, 1, 0)))
    ad = jnp.abs(dl)
    hit = (ad == 1) | (ad == 3) | (ad == 4)
    return pick(dl), pick(-dl), hit

def adj(x, y):
    ad = jnp.abs(x - y)
    return (ad == 1) | (ad == 3) | (ad == 4)

def select_scalars(p, i):
    s = jnp.where(p[0] == i, 0, jnp.where(p[1] == i, 1, jnp.where(p[2] == i, 2, 3)))
    pos = [jnp.where(s <= k, k + 1, k) for k in range(3)]
    nb = [jnp.where(s <= k, p[k + 1], p[k]) for k in range(3)]
    bsel = jnp.where(jnp.logical_not(adj(nb[1], nb[2])), 0, jnp.where(jnp.logical_not(adj(nb[0], nb[2])), 1, 2))
    def three(v):
        b = jnp.where(bsel == 0, v[0], jnp.where(bsel == 1, v[1], v[2]))
        a = jnp.where(bsel == 0, v[1], v[0])
        c = jnp.where(bsel == 2, v[1], v[2])
        return a, b, c
    return three(nb), three(pos), s

def setup_kernel(K, newton, nbr_ref, base_ref, t_ref, g_ref):
    base = base_ref[0]
    rows = []
    for w in range(2):
        i = base + 4 + w
        p = [nbr_ref[w, k] for k in range(4)]
        (a, b, c), pos, s = select_scalars(p, i)
        rows.append((i, a, b, c, pos, s))
    I = eye()
    def diag(j):
        q = j - base
        acc = None
        for k in range(4):
            x = t_ref[q, k]
            d = dg(x, x, 1, 1)
            acc = d if acc is None else acc + d
        return 2.0 * I + acc * (1.0 / 128)
    def off(x, y):
        tx, ty, hit = edge(y - x)
        sc = jnp.where(hit, 1.0 / 128, 0.0).astype(F32)
        return dg(t_ref[x - base, tx], t_ref[y - base, ty], 1, 1) * sc
    D = [[diag(j) for j in r[:4]] for r in rows]
    inv1 = inverses([D[0][1], D[0][3], D[1][1], D[1][3]], K, newton)
    st = []
    for w, r in enumerate(rows):
        i, a, b, c, pos, s = r
        Aia, Aib, Aic = off(i, a), off(i, b), off(i, c)
        Aab, Acb = off(a, b), off(c, b)
        P, Q = split(inv1[2*w]), split(inv1[2*w+1])
        sab, scb, sia, sic = split(Aab), split(Acb), split(Aia), split(Aic)
        Za, Zc = mm(sia, P), mm(sic, Q)
        Va, Vc = mm(P, sab), mm(Q, scb)
        sva, svc = split(Va), split(Vc)
        Sb = D[w][2] - mm(sab, sva, 0, 0) - mm(scb, svc, 0, 0)
        Aibp = Aib - mm(sia, sva) - mm(sic, svc)
        Aiip = D[w][0] - mm(split(Za), sia, 1, 1) - mm(split(Zc), sic, 1, 1)
        st.append((Za, Zc, sva, svc, Sb, Aibp, Aiip))
    inv2 = inverses([x[4] for x in st], K, newton)
    Ss, Ys = [], []
    for w in range(2):
        Za, Zc, sva, svc, Sb, Aibp, Aiip = st[w]
        sap = split(Aibp)
        Yb = mm(sap, split(inv2[w]))
        syb = split(Yb)
        Si = Aiip - mm(syb, sap, 1, 1)
        Ya = Za - mm(syb, sva, 1, 1)
        Yc = Zc - mm(syb, svc, 1, 1)
        Ss.append(Si); Ys.append((Ya, Yb, Yc))
    Us = uinv(Ss)
    for w in range(2):
        su = split(Us[w])
        i, a, b, c, pos, s = rows[w]
        for y, ps in zip(Ys[w], pos):
            g_ref[w, ps] = -mm(su, split(y))
        g_ref[w, s] = Us[w]

def setup_call(nbr, base, tiles, K=8, newton=1):
    return pl.pallas_call(
        functools.partial(setup_kernel, K, newton),
        out_shape=jax.ShapeDtypeStruct((2, 4, 128, 128), F32),
        in_specs=[pl.BlockSpec(memory_space=pltpu.SMEM), pl.BlockSpec(memory_space=pltpu.SMEM), pl.BlockSpec(memory_space=pltpu.VMEM)],
        out_specs=pl.BlockSpec(memory_space=pltpu.VMEM),
        compiler_params=pltpu.CompilerParams(vmem_limit_bytes=60*1024*1024),
    )(nbr, base, tiles)


def local(tile_factor, coupling, nbr_list, setup_slot, residual):
    rows, grp = lax.axis_size("rows"), lax.axis_size("grp")
    count = rows * grp
    both = ("rows", "grp")
    r = lax.axis_index("rows")
    g = lax.axis_index("grp")
    slab_start = r * NBR
    own = jnp.concatenate([coupling, tile_factor[:, None]], axis=1)

    def shifted(v, steps):
        return lax.ppermute(v, both, [(s, s + steps) for s in range(count) if 0 <= s + steps < count])

    tiles = jnp.concatenate([shifted(own, 2), shifted(own, 1), own, shifted(own, -1), shifted(own, -2)], axis=0)
    mine = lax.dynamic_slice_in_dim(nbr_list, 2 * g, 2, 0)
    base = (slab_start + 2 * g - 4).astype(jnp.int32).reshape(1)
    factor = setup_call(mine, base, tiles, 14, 1)
    slab_factor = lax.all_to_all(
        jnp.broadcast_to(factor[None], (grp, *factor.shape)), "grp", 0, 0, tiled=True
    ).reshape(NBR, PAT, B, B)
    slots = setup_slot[0]
    local_rows = jnp.arange(NBR, dtype=jnp.int32)
    by_slot = jnp.sum(jnp.where(slots[:, None] == local_rows[None, :], local_rows[:, None], 0), axis=0)
    out_rows = lax.dynamic_slice_in_dim(by_slot, 2 * g, 2)
    factor_rows = jnp.swapaxes(slab_factor[out_rows], 1, 2).reshape(2, B, PAT * B)

    columns = residual.shape[0]
    up = [(s, s + 1) for s in range(rows - 1)]
    down = [(s + 1, s) for s in range(rows - 1)]
    before = lax.ppermute(residual[:, 4 * B:], "rows", up)
    after = lax.ppermute(residual[:, : 4 * B], "rows", down)
    near = jnp.concatenate([before, residual, after], axis=1).reshape(columns, 16, B)
    places = nbr_list - slab_start + 4
    picked = near[:, places]
    high = lax.Precision.HIGHEST
    reduced = jnp.einsum("nabk,cnak->cnb", slab_factor, picked, precision=high)
    terms = jnp.einsum("nabk,cnb->cnak", slab_factor, reduced, precision=high)
    spread = (places.reshape(-1)[:, None] == jnp.arange(16, dtype=jnp.int32)[None, :]).astype(F32)
    summed = jnp.einsum("cpk,pe->cek", terms.reshape(columns, NBR * PAT, B), spread, precision=high)
    lower = summed[:, :4].astype(BF)
    upper = summed[:, 12:].astype(BF)
    from_next = lax.ppermute(lower, "rows", down).astype(F32)
    from_prev = lax.ppermute(upper, "rows", up).astype(F32)
    middle = summed[:, 4:12]
    result = middle + jnp.concatenate([from_prev, from_next], axis=1)
    return factor_rows, result.reshape(columns, NBR * B)


def solution(mesh):
    return jax.shard_map(
        local,
        mesh=mesh,
        in_specs=(
            P(("rows", "grp"), None, None),
            P(("rows", "grp"), None, None, None),
            P("rows", None),
            P("rows", None),
            P("grp", "rows"),
        ),
        out_specs=(P(("rows", "grp"), None, None), P("grp", "rows")),
        check_vma=False,
    )
```

```python
import functools

import jax
import jax.numpy as jnp
from jax import lax
from jax.experimental import pallas as pl
from jax.experimental.pallas import tpu as pltpu
from jax.sharding import PartitionSpec as P

F32 = jnp.float32
BF = jnp.bfloat16
MESH = pl.DeviceIdType.MESH
B = 128
PAT = 4
NBR = 8
REACH = (-4, -3, -1, 1, 3, 4)
DOUBLINGS = 15


def split(x):
    high = x.astype(BF)
    return high, (x - high.astype(F32)).astype(BF)


def dg(a, b, ca, cb):
    return lax.dot_general(a, b, (((ca,), (cb,)), ((), ())), preferred_element_type=F32)


def mm(a, b, ca=1, cb=0):
    return dg(a[0], b[0], ca, cb) + (dg(a[0], b[1], ca, cb) + dg(a[1], b[0], ca, cb))


def eye():
    shape = (B, B)
    return (lax.broadcasted_iota(jnp.int32, shape, 0) == lax.broadcasted_iota(jnp.int32, shape, 1)).astype(F32)


def inverses(mats):
    unit = eye()
    scales = []
    for mat in mats:
        norm = jnp.max(jnp.sum(jnp.abs(mat), axis=0, keepdims=True), axis=1, keepdims=True)
        scales.append(1.98 / norm)
    start = tuple((unit - mat * scale, unit) for mat, scale in zip(mats, scales))

    def double(_, state):
        new = []
        for power, series in state:
            ph, pl_ = split(power)
            sh, sl = split(series)
            first = jnp.concatenate([ph, sh], axis=1)
            out = dg(jnp.concatenate([ph, pl_], axis=1), jnp.concatenate([first, first], axis=0), 1, 0)
            out = out + dg(ph, jnp.concatenate([pl_, sl], axis=1), 1, 0)
            new.append((out[:, :B], series + out[:, B:]))
        return tuple(new)

    state = lax.fori_loop(0, DOUBLINGS, double, start)
    result = []
    for mat, scale, (_, series) in zip(mats, scales, state):
        guess = series * scale
        gs = split(guess)
        miss = unit - mm(split(mat), gs)
        result.append(guess + mm(gs, split(miss)))
    return result


def sweep(first, last, slabs):
    lane = lax.broadcasted_iota(jnp.int32, (1, B), 1)
    sub = lax.broadcasted_iota(jnp.int32, (8, 1), 0)

    def round_(it, state):
        done = []
        for mat in state:
            mat = list(mat)
            live = [(it <= p).astype(F32) for p in range(15)]
            for s in range(7, -1, -1):
                at = 120 + s
                row = mat[15][s:s + 1, :]
                pivot = row[:, at:at + 1]
                inv = 1.0 / pivot
                scaled = jnp.where(lane == at, 1.0 + inv, row * inv)
                for p in range(16):
                    c = mat[p][:, at:at + 1]
                    if p == 15:
                        if s == 0:
                            continue
                        c = jnp.where(sub < s, c, 0.0)
                    else:
                        c = c * live[p]
                    mat[p] = mat[p] - c * scaled
                final = jnp.where((lane >= 8 * it) & (lane < at), 0.0, jnp.where(lane == at, 1.0, row)) * lax.rsqrt(pivot)
                mat[15] = jnp.where(sub == s, final, mat[15])
            mat = [pltpu.roll(x, 8, 1) for x in mat]
            done.append(tuple([mat[15]] + mat[:15]))
        return tuple(done)

    return lax.fori_loop(first, last, round_, slabs)


def linked(x, y):
    gap = jnp.abs(x - y)
    return (gap == 1) | (gap == 3) | (gap == 4)


def tile_of(gap):
    return jnp.where(gap == 1, 1, jnp.where((gap == 3) | (gap == 4), 2, jnp.where(gap == -3, 1, 0)))


def order(p, i):
    s = jnp.where(p[0] == i, 0, jnp.where(p[1] == i, 1, jnp.where(p[2] == i, 2, 3)))
    pos = [jnp.where(s <= k, k + 1, k) for k in range(3)]
    nb = [jnp.where(s <= k, p[k + 1], p[k]) for k in range(3)]
    mid = jnp.where(linked(nb[1], nb[2]), jnp.where(linked(nb[0], nb[2]), 2, 1), 0)

    def three(v):
        b = jnp.where(mid == 0, v[0], jnp.where(mid == 1, v[1], v[2]))
        return jnp.where(mid == 0, v[1], v[0]), b, jnp.where(mid == 2, v[1], v[2])

    return three(nb), three(pos), s


def kernel(rows, nbr, slot, tf, cp, res, out_f, out_x, near, yall, uall, x3, acc, tsend, trecv,
           own_sem, x_sem, near_send, near_recv, y_send, y_recv, u_send, u_recv, t_sem, xr_sem):
    r = lax.axis_index("rows")
    g = lax.axis_index("grp")
    m = r * 4 + g
    count = rows * 4
    after = lax.rem(m + 1, count)
    before = lax.rem(m + count - 1, count)
    nxt = (after // 4, lax.rem(after, 4))
    prv = (before // 4, lax.rem(before, 4))
    up = (lax.rem(r + 1, rows), g)
    down = (lax.rem(r + rows - 1, rows), g)
    right = (r, lax.rem(g + 1, 4))
    left = (r, lax.rem(g + 3, 4))

    def remote(src, dst, ssem, rsem, dev):
        return pltpu.make_async_remote_copy(
            src_ref=src, dst_ref=dst, send_sem=ssem, recv_sem=rsem, device_id=dev, device_id_type=MESH)

    own = [pltpu.make_async_copy(cp.at[w], near.at[4 + w, pl.ds(0, 3)], own_sem.at[w]) for w in range(2)]
    own += [pltpu.make_async_copy(tf.at[w], near.at[4 + w, 3], own_sem.at[2 + w]) for w in range(2)]
    own += [pltpu.make_async_copy(res.at[:, pl.ds(B * e, B)], x3.at[4 + e], x_sem.at[e]) for e in range(8)]
    for copy in own:
        copy.start()

    barrier = pltpu.get_barrier_semaphore()
    for dev in (nxt, prv, up, down, right, left):
        pl.semaphore_signal(barrier, inc=1, device_id=dev, device_id_type=MESH)
    pl.semaphore_wait(barrier, 6)

    def source(w, t):
        return cp.at[w, t] if t < 3 else tf.at[w]

    sends = []

    def send(src, q, t, dev, lane):
        copy = remote(src, near.at[q, t], near_send.at[lane, t], near_recv.at[q, t], dev)
        copy.start()
        sends.append(copy)

    def arrived(q, t):
        remote(near.at[q, t], near.at[q, t], near_send.at[0, t], near_recv.at[q, t], nxt).wait_recv()

    for t in range(4):
        send(source(0, t), 2, t, nxt, 0)
        send(source(1, t), 7, t, prv, 1)
    for t in range(4):
        send(source(1, t), 3, t, nxt, 2)
        send(source(0, t), 6, t, prv, 3)
    halo = []
    for e in range(4):
        halo.append(remote(res.at[:, pl.ds(B * (4 + e), B)], x3.at[e], xr_sem.at[0, e], xr_sem.at[1, e], up))
        halo.append(remote(res.at[:, pl.ds(B * e, B)], x3.at[12 + e], xr_sem.at[2, e], xr_sem.at[3, e], down))
    for t in range(4):
        arrived(2, t)
        send(near.at[2, t], 0, t, nxt, 4)
        arrived(7, t)
        send(near.at[7, t], 9, t, prv, 5)
    for t in range(4):
        arrived(0, t)
        send(near.at[0, t], 8, t, down, 6)
        arrived(9, t)
        send(near.at[9, t], 1, t, up, 7)
    for copy in halo:
        copy.start()
    for copy in own:
        copy.wait()
    for t in range(4):
        for q in (3, 6, 8, 1):
            arrived(q, t)

    base = 2 * m - 4
    unit = eye()

    def picks(t):
        return order([nbr[t, k] for k in range(PAT)], NBR * r + t)

    def place(j):
        return jnp.clip(j - base, 0, 9)

    def diag(j):
        total = None
        for k in range(4):
            tile = near[place(j), k]
            part = dg(tile, tile, 1, 1)
            total = part if total is None else total + part
        return 2.0 * unit + total * (1.0 / B)

    def off(x, y):
        scale = jnp.where(linked(x, y), 1.0 / B, 0.0).astype(F32)
        return dg(near[place(x), tile_of(y - x)], near[place(y), tile_of(x - y)], 1, 1) * scale

    mine = [2 * g + w for w in range(2)]
    nodes = [picks(t)[0] for t in mine]
    ends = inverses([diag(nodes[w][k]) for w in range(2) for k in (0, 2)])
    held = []
    for w in range(2):
        i = NBR * r + mine[w]
        a, b, c = nodes[w]
        ia, ib, ic = split(off(i, a)), off(i, b), split(off(i, c))
        ab, cb = split(off(a, b)), split(off(c, b))
        inv_a, inv_c = split(ends[2 * w]), split(ends[2 * w + 1])
        za, zc = mm(ia, inv_a), mm(ic, inv_c)
        va, vc = split(mm(inv_a, ab)), split(mm(inv_c, cb))
        schur = diag(b) - mm(ab, va, 0, 0) - mm(cb, vc, 0, 0)
        rest_ib = ib - mm(ia, va) - mm(ic, vc)
        rest_ii = diag(i) - mm(split(za), ia, 1, 1) - mm(split(zc), ic, 1, 1)
        held.append((za, zc, va, vc, schur, rest_ib, rest_ii))
    mids = inverses([h[4] for h in held])
    tops = []
    for w in range(2):
        za, zc, va, vc, _, rest_ib, rest_ii = held[w]
        rs = split(rest_ib)
        yb = mm(rs, split(mids[w]))
        ys = split(yb)
        yall[mine[w], 0] = za - mm(ys, va, 1, 1)
        yall[mine[w], 1] = yb
        yall[mine[w], 2] = zc - mm(ys, vc, 1, 1)
        tops.append(rest_ii - mm(ys, rs, 1, 1))

    def y_copy(t, k, dev, lane):
        return remote(yall.at[t, k], yall.at[t, k], y_send.at[lane, k], y_recv.at[t, k], dev)

    def u_copy(t, dev, lane):
        return remote(uall.at[t], uall.at[t], u_send.at[lane], u_recv.at[t], dev)

    from_left = 2 * lax.rem(g + 3, 4)
    from_right = 2 * lax.rem(g + 1, 4)
    across = 2 * lax.rem(g + 2, 4)
    y_sends = []
    for k in range(3):
        y_sends += [y_copy(mine[0], k, right, 0), y_copy(mine[1], k, left, 1)]
    for k in range(3):
        y_sends += [y_copy(mine[1], k, right, 2), y_copy(mine[0], k, left, 3)]
    for copy in y_sends:
        copy.start()

    slabs = tuple(tuple(top[8 * p:8 * p + 8, :] for p in range(16)) for top in tops)
    for part in range(4):
        slabs = sweep(4 * part, 4 * part + 4, slabs)
        if part < 3:
            y_copy(from_left, part, right, 0).wait_recv()
            copy = y_copy(from_left, part, right, 4)
            copy.start()
            y_sends.append(copy)
            y_copy(from_right + 1, part, left, 0).wait_recv()
            copy = y_copy(from_right + 1, part, left, 5)
            copy.start()
            y_sends.append(copy)
    for w in range(2):
        uall[mine[w]] = jnp.concatenate(slabs[w], axis=0)
    u_sends = [u_copy(mine[0], right, 0), u_copy(mine[1], left, 1), u_copy(mine[1], right, 2), u_copy(mine[0], left, 3)]
    for copy in u_sends:
        copy.start()

    acc[...] = jnp.zeros_like(acc)
    for copy in halo:
        copy.wait()

    def gather(t):
        ids, _, _ = picks(t)
        x = jnp.concatenate([x3[jnp.clip(j - (NBR * r - 4), 0, 15)] for j in ids], axis=1)
        y = jnp.concatenate([yall[t, k] for k in range(3)], axis=1)
        ysp = split(y)
        return x3[4 + t] - mm(split(x), ysp, 1, 1)

    def spread(t, v):
        ids, _, _ = picks(t)
        u = split(uall[t])
        w = mm(split(mm(split(v), u, 1, 1)), u)
        y = jnp.concatenate([yall[t, k] for k in range(3)], axis=1)
        terms = mm(split(w), split(y))
        acc[4 + t] += w
        for gap in REACH:
            part = None
            for k in range(3):
                weight = jnp.where(ids[k] == NBR * r + t + gap, 1.0, 0.0).astype(F32)
                term = terms[:, B * k:B * k + B] * weight
                part = term if part is None else part + term
            acc[4 + t + gap] -= part

    vs = [gather(t) for t in mine]
    u_copy(from_left, right, 0).wait_recv()
    copy = u_copy(from_left, right, 4)
    copy.start()
    u_sends.append(copy)
    u_copy(from_right + 1, left, 0).wait_recv()
    copy = u_copy(from_right + 1, left, 5)
    copy.start()
    u_sends.append(copy)
    for t, v in zip(mine, vs):
        spread(t, v)
    others = [from_left, from_right + 1, from_left + 1, from_right]
    for t in others[2:]:
        for k in range(3):
            y_copy(t, k, right, 0).wait_recv()
        u_copy(t, right, 0).wait_recv()
    for t in others:
        spread(t, gather(t))
    for t in (across, across + 1):
        for k in range(3):
            y_copy(t, k, right, 0).wait_recv()
    vs = [gather(t) for t in (across, across + 1)]
    for t, v in zip((across, across + 1), vs):
        u_copy(t, right, 0).wait_recv()
        spread(t, v)

    for e in range(4):
        tsend[0, e] = acc[e].astype(BF)
        tsend[1, e] = acc[12 + e].astype(BF)
    swaps = [remote(tsend.at[0], trecv.at[0], t_sem.at[0], t_sem.at[1], down),
             remote(tsend.at[1], trecv.at[1], t_sem.at[2], t_sem.at[3], up)]
    for copy in swaps:
        copy.start()

    for w in range(2):
        t = 0
        for k in range(NBR):
            t = t + jnp.where(slot[0, k] == 2 * g + w, k, 0)
        t = jnp.minimum(t, NBR - 1)
        _, pos, s = picks(t)
        u = uall[t]
        us = split(u)
        for a in range(PAT):
            k = jnp.where(pos[1] == a, 1, jnp.where(pos[2] == a, 2, 0))
            self_ = (s == a).astype(F32)
            out_f[w, :, B * a:B * a + B] = u * self_ - mm(us, split(yall[t, k])) * (1.0 - self_)

    for copy in swaps:
        copy.wait()
    for e in range(4):
        out_x[:, B * e:B * e + B] = acc[4 + e] + trecv[1, e].astype(F32)
        out_x[:, B * (4 + e):B * (4 + e) + B] = acc[8 + e] + trecv[0, e].astype(F32)
    for copy in sends + y_sends + u_sends:
        copy.wait_send()


def solution(mesh):
    rows = mesh.shape["rows"]
    smem = pl.BlockSpec(memory_space=pltpu.SMEM)
    raw = pl.BlockSpec(memory_space=pl.ANY)
    whole = pl.BlockSpec(memory_space=pltpu.VMEM)

    def local(tile_factor, coupling, nbr_list, setup_slot, residual):
        columns = residual.shape[0]
        dma = pltpu.SemaphoreType.DMA
        factor, result = pl.pallas_call(
            functools.partial(kernel, rows),
            out_shape=(
                jax.ShapeDtypeStruct((2, B, PAT * B), F32),
                jax.ShapeDtypeStruct((columns, NBR * B), F32),
            ),
            in_specs=[smem, smem, raw, raw, raw],
            out_specs=(whole, whole),
            scratch_shapes=[
                pltpu.VMEM((10, 4, B, B), BF),
                pltpu.VMEM((NBR, 3, B, B), F32),
                pltpu.VMEM((NBR, B, B), F32),
                pltpu.VMEM((16, columns, B), F32),
                pltpu.VMEM((16, columns, B), F32),
                pltpu.VMEM((2, 4, columns, B), BF),
                pltpu.VMEM((2, 4, columns, B), BF),
                dma((4,)), dma((8,)), dma((8, 4)), dma((10, 4)), dma((6, 3)), dma((NBR, 3)),
                dma((6,)), dma((NBR,)), dma((4,)), dma((4, 4)),
            ],
            compiler_params=pltpu.CompilerParams(
                collective_id=0, has_side_effects=True, vmem_limit_bytes=48 * 1024 * 1024
            ),
        )(nbr_list, setup_slot, tile_factor, coupling, residual)
        return factor, result

    return jax.shard_map(
        local,
        mesh=mesh,
        in_specs=(
            P(("rows", "grp"), None, None),
            P(("rows", "grp"), None, None, None),
            P("rows", None),
            P("rows", None),
            P("grp", "rows"),
        ),
        out_specs=(P(("rows", "grp"), None, None), P("grp", "rows")),
        check_vma=False,
    )
```

```python
import functools

import jax
import jax.numpy as jnp
from jax import lax
from jax.experimental import pallas as pl
from jax.experimental.pallas import tpu as pltpu
from jax.sharding import PartitionSpec as P

F32 = jnp.float32
BF = jnp.bfloat16
MESH = pl.DeviceIdType.MESH
B = 128
PAT = 4
NBR = 8
REACH = (-4, -3, -1, 1, 3, 4)
DOUBLINGS = 15


def split(x):
    high = x.astype(BF)
    return high, (x - high.astype(F32)).astype(BF)


def dg(a, b, ca, cb):
    return lax.dot_general(a, b, (((ca,), (cb,)), ((), ())), preferred_element_type=F32)


def mm(a, b, ca=1, cb=0):
    return dg(a[0], b[0], ca, cb) + (dg(a[0], b[1], ca, cb) + dg(a[1], b[0], ca, cb))


def eye():
    shape = (B, B)
    return (lax.broadcasted_iota(jnp.int32, shape, 0) == lax.broadcasted_iota(jnp.int32, shape, 1)).astype(F32)


def inverses(mats):
    unit = eye()
    scales = []
    for mat in mats:
        norm = jnp.max(jnp.sum(jnp.abs(mat), axis=0, keepdims=True), axis=1, keepdims=True)
        scales.append(1.98 / norm)
    start = tuple((unit - mat * scale, unit) for mat, scale in zip(mats, scales))

    def double(_, state):
        new = []
        for power, series in state:
            ph, pl_ = split(power)
            sh, sl = split(series)
            first = jnp.concatenate([ph, sh], axis=1)
            out = dg(jnp.concatenate([ph, pl_], axis=1), jnp.concatenate([first, first], axis=0), 1, 0)
            out = out + dg(ph, jnp.concatenate([pl_, sl], axis=1), 1, 0)
            new.append((out[:, :B], series + out[:, B:]))
        return tuple(new)

    state = lax.fori_loop(0, DOUBLINGS, double, start)
    result = []
    for mat, scale, (_, series) in zip(mats, scales, state):
        guess = series * scale
        gs = split(guess)
        miss = unit - mm(split(mat), gs)
        result.append(guess + mm(gs, split(miss)))
    return result


def sweep(first, last, slabs):
    lane = lax.broadcasted_iota(jnp.int32, (1, B), 1)
    sub = lax.broadcasted_iota(jnp.int32, (8, 1), 0)

    def round_(it, state):
        done = []
        for mat in state:
            mat = list(mat)
            live = [(it <= p).astype(F32) for p in range(15)]
            for s in range(7, -1, -1):
                at = 120 + s
                row = mat[15][s:s + 1, :]
                pivot = row[:, at:at + 1]
                inv = 1.0 / pivot
                scaled = jnp.where(lane == at, 1.0 + inv, row * inv)
                for p in range(16):
                    c = mat[p][:, at:at + 1]
                    if p == 15:
                        if s == 0:
                            continue
                        c = jnp.where(sub < s, c, 0.0)
                    else:
                        c = c * live[p]
                    mat[p] = mat[p] - c * scaled
                final = jnp.where((lane >= 8 * it) & (lane < at), 0.0, jnp.where(lane == at, 1.0, row)) * lax.rsqrt(pivot)
                mat[15] = jnp.where(sub == s, final, mat[15])
            mat = [pltpu.roll(x, 8, 1) for x in mat]
            done.append(tuple([mat[15]] + mat[:15]))
        return tuple(done)

    return lax.fori_loop(first, last, round_, slabs)


def linked(x, y):
    gap = jnp.abs(x - y)
    return (gap == 1) | (gap == 3) | (gap == 4)


def tile_of(gap):
    return jnp.where(gap == 1, 1, jnp.where((gap == 3) | (gap == 4), 2, jnp.where(gap == -3, 1, 0)))


def order(p, i):
    s = jnp.where(p[0] == i, 0, jnp.where(p[1] == i, 1, jnp.where(p[2] == i, 2, 3)))
    pos = [jnp.where(s <= k, k + 1, k) for k in range(3)]
    nb = [jnp.where(s <= k, p[k + 1], p[k]) for k in range(3)]
    mid = jnp.where(linked(nb[1], nb[2]), jnp.where(linked(nb[0], nb[2]), 2, 1), 0)

    def three(v):
        b = jnp.where(mid == 0, v[0], jnp.where(mid == 1, v[1], v[2]))
        return jnp.where(mid == 0, v[1], v[0]), b, jnp.where(mid == 2, v[1], v[2])

    return three(nb), three(pos), s


def kernel(rows, nbr, slot, tf, cp, res, out_f, out_x, near, yall, uall, x3, acc, tsend, trecv,
           own_sem, x_sem, near_send, near_recv, y_send, y_recv, u_send, u_recv, t_sem, xr_sem):
    r = lax.axis_index("rows")
    g = lax.axis_index("grp")
    m = r * 4 + g
    count = rows * 4
    has_nxt, has_prv = m < count - 1, m > 0
    has_up, has_down = r < rows - 1, r > 0
    inner = has_nxt & has_prv
    after = jnp.minimum(m + 1, count - 1)
    before = jnp.maximum(m - 1, 0)
    nxt = (after // 4, lax.rem(after, 4))
    prv = (before // 4, lax.rem(before, 4))
    up = (jnp.minimum(r + 1, rows - 1), g)
    down = (jnp.maximum(r - 1, 0), g)
    right = (r, lax.rem(g + 1, 4))
    left = (r, lax.rem(g + 3, 4))

    def when(there, act):
        if there is None:
            act()
        else:
            pl.when(there)(act)

    def remote(src, dst, ssem, rsem, dev):
        return pltpu.make_async_remote_copy(
            src_ref=src, dst_ref=dst, send_sem=ssem, recv_sem=rsem, device_id=dev, device_id_type=MESH)

    own = [pltpu.make_async_copy(cp.at[w], near.at[4 + w, pl.ds(0, 3)], own_sem.at[w]) for w in range(2)]
    own += [pltpu.make_async_copy(tf.at[w], near.at[4 + w, 3], own_sem.at[2 + w]) for w in range(2)]
    own += [pltpu.make_async_copy(res.at[:, pl.ds(B * e, B)], x3.at[4 + e], x_sem.at[e]) for e in range(8)]
    for copy in own:
        copy.start()

    def blank(side):
        trecv[side] = jnp.zeros_like(trecv[side])

    when(r == rows - 1, lambda: blank(0))
    when(r == 0, lambda: blank(1))
    barrier = pltpu.get_barrier_semaphore()
    for there, dev in ((has_nxt, nxt), (has_prv, prv), (has_up, up), (has_down, down), (None, right), (None, left)):
        when(there, lambda: pl.semaphore_signal(barrier, inc=1, device_id=dev, device_id_type=MESH))
    partners = 2
    for there in (has_nxt, has_prv, has_up, has_down):
        partners = partners + there.astype(jnp.int32)
    pl.semaphore_wait(barrier, partners)

    def source(w, t):
        return cp.at[w, t] if t < 3 else tf.at[w]

    sends = []

    def send(there, src, q, t, dev, lane):
        copy = remote(src, near.at[q, t], near_send.at[lane, t], near_recv.at[q, t], dev)
        when(there, copy.start)
        sends.append((there, copy))

    def arrived(there, q, t):
        when(there, remote(near.at[q, t], near.at[q, t], near_send.at[0, t], near_recv.at[q, t], nxt).wait_recv)

    for t in range(4):
        send(has_nxt, source(0, t), 2, t, nxt, 0)
        send(has_prv, source(1, t), 7, t, prv, 1)
    for t in range(4):
        send(has_nxt, source(1, t), 3, t, nxt, 2)
        send(has_prv, source(0, t), 6, t, prv, 3)
    halo = []
    for e in range(4):
        halo.append((has_up, has_down, remote(res.at[:, pl.ds(B * (4 + e), B)], x3.at[e], xr_sem.at[0, e], xr_sem.at[1, e], up)))
        halo.append((has_down, has_up, remote(res.at[:, pl.ds(B * e, B)], x3.at[12 + e], xr_sem.at[2, e], xr_sem.at[3, e], down)))
    middle = (g == 1) | (g == 2)
    first_slab, last_slab = middle & (r == 0), middle & (r == rows - 1)
    for t in range(4):
        arrived(has_prv, 2, t)
        send(inner, near.at[2, t], 0, t, nxt, 4)
        arrived(has_nxt, 7, t)
        send(inner, near.at[7, t], 9, t, prv, 5)
    for t in range(4):
        arrived(has_prv, 3, t)
        send(first_slab, near.at[3, t], 1, t, nxt, 8)
        arrived(has_nxt, 6, t)
        send(last_slab, near.at[6, t], 8, t, prv, 9)
    for t in range(4):
        arrived(m > 1, 0, t)
        send(has_down, near.at[0, t], 8, t, down, 6)
        arrived(m < count - 2, 9, t)
        send(has_up, near.at[9, t], 1, t, up, 7)
    for there, _, copy in halo:
        when(there, copy.start)
    for copy in own:
        copy.wait()
    for t in range(4):
        arrived(m < count - 2, 8, t)
        arrived(m > 1, 1, t)

    base = 2 * m - 4
    unit = eye()

    def picks(t):
        return order([nbr[k, t] for k in range(PAT)], NBR * r + t)

    def place(j):
        return jnp.clip(j - base, 0, 9)

    def diag(j):
        total = None
        for k in range(4):
            tile = near[place(j), k]
            part = dg(tile, tile, 1, 1)
            total = part if total is None else total + part
        return 2.0 * unit + total * (1.0 / B)

    def off(x, y):
        scale = jnp.where(linked(x, y), 1.0 / B, 0.0).astype(F32)
        return dg(near[place(x), tile_of(y - x)], near[place(y), tile_of(x - y)], 1, 1) * scale

    mine = [2 * g + w for w in range(2)]
    nodes = [picks(t)[0] for t in mine]
    ends = inverses([diag(nodes[w][k]) for w in range(2) for k in (0, 2)])
    held = []
    for w in range(2):
        i = NBR * r + mine[w]
        a, b, c = nodes[w]
        ia, ib, ic = split(off(i, a)), off(i, b), split(off(i, c))
        ab, cb = split(off(a, b)), split(off(c, b))
        inv_a, inv_c = split(ends[2 * w]), split(ends[2 * w + 1])
        za, zc = mm(ia, inv_a), mm(ic, inv_c)
        va, vc = split(mm(inv_a, ab)), split(mm(inv_c, cb))
        schur = diag(b) - mm(ab, va, 0, 0) - mm(cb, vc, 0, 0)
        rest_ib = ib - mm(ia, va) - mm(ic, vc)
        rest_ii = diag(i) - mm(split(za), ia, 1, 1) - mm(split(zc), ic, 1, 1)
        held.append((za, zc, va, vc, schur, rest_ib, rest_ii))
    mids = inverses([h[4] for h in held])
    tops = []
    for w in range(2):
        za, zc, va, vc, _, rest_ib, rest_ii = held[w]
        rs = split(rest_ib)
        yb = mm(rs, split(mids[w]))
        ys = split(yb)
        yall[mine[w], 0] = za - mm(ys, va, 1, 1)
        yall[mine[w], 1] = yb
        yall[mine[w], 2] = zc - mm(ys, vc, 1, 1)
        tops.append(rest_ii - mm(ys, rs, 1, 1))

    def y_copy(t, k, dev, lane):
        return remote(yall.at[t, k], yall.at[t, k], y_send.at[lane, k], y_recv.at[t, k], dev)

    def u_copy(t, dev, lane):
        return remote(uall.at[t], uall.at[t], u_send.at[lane], u_recv.at[t], dev)

    from_left = 2 * lax.rem(g + 3, 4)
    from_right = 2 * lax.rem(g + 1, 4)
    across = 2 * lax.rem(g + 2, 4)
    y_sends = []
    for k in range(3):
        y_sends += [y_copy(mine[0], k, right, 0), y_copy(mine[1], k, left, 1)]
    for k in range(3):
        y_sends += [y_copy(mine[1], k, right, 2), y_copy(mine[0], k, left, 3)]
    for copy in y_sends:
        copy.start()

    slabs = tuple(tuple(top[8 * p:8 * p + 8, :] for p in range(16)) for top in tops)
    for part in range(4):
        slabs = sweep(4 * part, 4 * part + 4, slabs)
        if part < 3:
            y_copy(from_left, part, right, 0).wait_recv()
            copy = y_copy(from_left, part, right, 4)
            copy.start()
            y_sends.append(copy)
            y_copy(from_right + 1, part, left, 0).wait_recv()
            copy = y_copy(from_right + 1, part, left, 5)
            copy.start()
            y_sends.append(copy)
    for w in range(2):
        uall[mine[w]] = jnp.concatenate(slabs[w], axis=0)
    u_sends = [u_copy(mine[0], right, 0), u_copy(mine[1], left, 1), u_copy(mine[1], right, 2), u_copy(mine[0], left, 3)]
    for copy in u_sends:
        copy.start()

    acc[...] = jnp.zeros_like(acc)
    for there, back, copy in halo:
        when(there, copy.wait_send)
        when(back, copy.wait_recv)

    def gather(t):
        ids, _, _ = picks(t)
        x = jnp.concatenate([x3[jnp.clip(j - (NBR * r - 4), 0, 15)] for j in ids], axis=1)
        y = jnp.concatenate([yall[t, k] for k in range(3)], axis=1)
        ysp = split(y)
        return x3[4 + t] - mm(split(x), ysp, 1, 1)

    def spread(t, v):
        ids, _, _ = picks(t)
        u = split(uall[t])
        w = mm(split(mm(split(v), u, 1, 1)), u)
        y = jnp.concatenate([yall[t, k] for k in range(3)], axis=1)
        terms = mm(split(w), split(y))
        acc[4 + t] += w
        for gap in REACH:
            part = None
            for k in range(3):
                weight = jnp.where(ids[k] == NBR * r + t + gap, 1.0, 0.0).astype(F32)
                term = terms[:, B * k:B * k + B] * weight
                part = term if part is None else part + term
            acc[4 + t + gap] -= part

    vs = [gather(t) for t in mine]
    u_copy(from_left, right, 0).wait_recv()
    copy = u_copy(from_left, right, 4)
    copy.start()
    u_sends.append(copy)
    u_copy(from_right + 1, left, 0).wait_recv()
    copy = u_copy(from_right + 1, left, 5)
    copy.start()
    u_sends.append(copy)
    for t, v in zip(mine, vs):
        spread(t, v)
    others = [from_left, from_right + 1, from_left + 1, from_right]
    for t in others[2:]:
        for k in range(3):
            y_copy(t, k, right, 0).wait_recv()
        u_copy(t, right, 0).wait_recv()
    for t in others:
        spread(t, gather(t))
    for t in (across, across + 1):
        for k in range(3):
            y_copy(t, k, right, 0).wait_recv()
    vs = [gather(t) for t in (across, across + 1)]
    for t, v in zip((across, across + 1), vs):
        u_copy(t, right, 0).wait_recv()
        spread(t, v)

    for e in range(4):
        tsend[0, e] = acc[e].astype(BF)
        tsend[1, e] = acc[12 + e].astype(BF)
    swaps = [(has_down, has_up, remote(tsend.at[0], trecv.at[0], t_sem.at[0], t_sem.at[1], down)),
             (has_up, has_down, remote(tsend.at[1], trecv.at[1], t_sem.at[2], t_sem.at[3], up))]
    for there, _, copy in swaps:
        when(there, copy.start)

    for w in range(2):
        t = 0
        for k in range(NBR):
            t = t + jnp.where(slot[0, k] == 2 * g + w, k, 0)
        t = jnp.minimum(t, NBR - 1)
        _, pos, s = picks(t)
        u = uall[t]
        us = split(u)
        for a in range(PAT):
            k = jnp.where(pos[1] == a, 1, jnp.where(pos[2] == a, 2, 0))
            self_ = (s == a).astype(F32)
            out_f[w, :, B * a:B * a + B] = u * self_ - mm(us, split(yall[t, k])) * (1.0 - self_)

    for there, back, copy in swaps:
        when(there, copy.wait_send)
        when(back, copy.wait_recv)
    for e in range(4):
        out_x[:, B * e:B * e + B] = acc[4 + e] + trecv[1, e].astype(F32)
        out_x[:, B * (4 + e):B * (4 + e) + B] = acc[8 + e] + trecv[0, e].astype(F32)
    for there, copy in sends:
        when(there, copy.wait_send)
    for copy in y_sends + u_sends:
        copy.wait_send()


def solution(mesh):
    rows = mesh.shape["rows"]
    smem = pl.BlockSpec(memory_space=pltpu.SMEM)
    raw = pl.BlockSpec(memory_space=pltpu.HBM)
    whole = pl.BlockSpec(memory_space=pltpu.VMEM)

    def local(tile_factor, coupling, nbr_list, setup_slot, residual):
        columns = residual.shape[0]
        dma = pltpu.SemaphoreType.DMA
        factor, result = pl.pallas_call(
            functools.partial(kernel, rows),
            out_shape=(
                jax.ShapeDtypeStruct((2, B, PAT * B), F32),
                jax.ShapeDtypeStruct((columns, NBR * B), F32),
            ),
            in_specs=[smem, smem, raw, raw, raw],
            out_specs=(whole, whole),
            scratch_shapes=[
                pltpu.VMEM((10, 4, B, B), BF),
                pltpu.VMEM((NBR, 3, B, B), F32),
                pltpu.VMEM((NBR, B, B), F32),
                pltpu.VMEM((16, columns, B), F32),
                pltpu.VMEM((16, columns, B), F32),
                pltpu.VMEM((2, 4, columns, B), BF),
                pltpu.VMEM((2, 4, columns, B), BF),
                dma((4,)), dma((8,)), dma((10, 4)), dma((10, 4)), dma((6, 3)), dma((NBR, 3)),
                dma((6,)), dma((NBR,)), dma((4,)), dma((4, 4)),
            ],
            compiler_params=pltpu.CompilerParams(
                collective_id=0, has_side_effects=True, vmem_limit_bytes=67043328
            ),
        )(nbr_list.T, setup_slot, tile_factor, coupling, residual)
        return factor, result

    return jax.shard_map(
        local,
        mesh=mesh,
        in_specs=(
            P(("rows", "grp"), None, None),
            P(("rows", "grp"), None, None, None),
            P("rows", None),
            P("rows", None),
            P("grp", "rows"),
        ),
        out_specs=(P(("rows", "grp"), None, None), P("grp", "rows")),
        check_vma=False,
    )
```

```python
import functools

import jax
import jax.numpy as jnp
from jax import lax
from jax.experimental import pallas as pl
from jax.experimental.pallas import tpu as pltpu
from jax.sharding import PartitionSpec as P

F32 = jnp.float32
BF = jnp.bfloat16
MESH = pl.DeviceIdType.MESH
B = 128
PAT = 4
NBR = 8
REACH = (-4, -3, -1, 1, 3, 4)
DOUBLINGS = 9
HALF = 64


def split(x):
    high = x.astype(BF)
    return high, (x - high.astype(F32)).astype(BF)


def dg(a, b, ca, cb):
    return lax.dot_general(a, b, (((ca,), (cb,)), ((), ())), preferred_element_type=F32)


def mm(a, b, ca=1, cb=0):
    return dg(a[0], b[0], ca, cb) + (dg(a[0], b[1], ca, cb) + dg(a[1], b[0], ca, cb))


def eye(n=B):
    shape = (n, n)
    return (lax.broadcasted_iota(jnp.int32, shape, 0) == lax.broadcasted_iota(jnp.int32, shape, 1)).astype(F32)


def inverses(mats):
    size = mats[0].shape[0]
    unit = eye(size)
    start = []
    for mat in mats:
        norm = jnp.max(jnp.sum(jnp.abs(mat), axis=0, keepdims=True), axis=1, keepdims=True)
        scale = 2.0 / (2.0 + norm)
        start.append((unit - mat * scale, unit * scale, 2.0 * scale))

    def double(_, state):
        new = []
        for power, series, low in state:
            ph, pl_ = split(power)
            sh, sl = split(series)
            gain = low * (2.0 - low)
            s = 2.0 / (1.0 + gain)
            if size == B:
                first = jnp.concatenate([ph, sh], axis=1)
                out = dg(jnp.concatenate([ph, pl_], axis=1), jnp.concatenate([first, first], axis=0), 1, 0)
                out = out + dg(ph, jnp.concatenate([pl_, sl], axis=1), 1, 0)
                square, step = out[:, :B], out[:, B:]
            else:
                square, step = mm((ph, pl_), (ph, pl_)), mm((ph, pl_), (sh, sl))
            new.append((square * s + unit * (1.0 - s), (series + step) * s, gain * s))
        return tuple(new)

    state = lax.fori_loop(0, DOUBLINGS, double, tuple(start))
    result = []
    for mat, (_, guess, _) in zip(mats, state):
        gs = split(guess)
        miss = unit - mm(split(mat), gs)
        result.append(guess + mm(gs, split(miss)))
    return result


def sweep(mats):
    lane = lax.broadcasted_iota(jnp.int32, (1, B), 1)
    sub = lax.broadcasted_iota(jnp.int32, (8, 1), 0)

    def round_(it, state):
        done = []
        for mat in state:
            mat = list(mat)
            live = [(it <= p).astype(F32) for p in range(7)]
            for s in range(7, -1, -1):
                at = 120 + s
                row = mat[7][s:s + 1, :]
                pivot = row[:, at:at + 1]
                inv = 1.0 / pivot
                scaled = jnp.where(lane == at, 1.0 + inv, row * inv)
                for p in range(8):
                    c = mat[p][:, at:at + 1]
                    if p == 7:
                        if s == 0:
                            continue
                        c = jnp.where(sub < s, c, 0.0)
                    else:
                        c = c * live[p]
                    mat[p] = mat[p] - c * scaled
                final = jnp.where((lane >= 8 * it) & (lane < at), 0.0, jnp.where(lane == at, 1.0, row)) * lax.rsqrt(pivot)
                mat[7] = jnp.where(sub == s, final, mat[7])
            mat = [pltpu.roll(x, 8, 1) for x in mat]
            done.append(tuple([mat[7]] + mat[:7]))
        return tuple(done)

    slabs = lax.fori_loop(0, 8, round_, tuple(tuple(x[8 * p:8 * p + 8, :] for p in range(8)) for x in mats))
    return [jnp.concatenate(x, axis=0) for x in slabs]


def linked(x, y):
    gap = jnp.abs(x - y)
    return (gap == 1) | (gap == 3) | (gap == 4)


def tile_of(gap):
    return jnp.where(gap == 1, 1, jnp.where((gap == 3) | (gap == 4), 2, jnp.where(gap == -3, 1, 0)))


def order(p, i):
    s = jnp.where(p[0] == i, 0, jnp.where(p[1] == i, 1, jnp.where(p[2] == i, 2, 3)))
    pos = [jnp.where(s <= k, k + 1, k) for k in range(3)]
    nb = [jnp.where(s <= k, p[k + 1], p[k]) for k in range(3)]
    mid = jnp.where(linked(nb[1], nb[2]), jnp.where(linked(nb[0], nb[2]), 2, 1), 0)

    def three(v):
        b = jnp.where(mid == 0, v[0], jnp.where(mid == 1, v[1], v[2]))
        return jnp.where(mid == 0, v[1], v[0]), b, jnp.where(mid == 2, v[1], v[2])

    return three(nb), three(pos), s


def kernel(rows, nbr, slot, tf, cp, res, out_f, out_x, near, yall, uall, x3, acc, tsend, trecv,
           own_sem, x_sem, near_send, near_recv, y_send, y_recv, u_send, u_recv, t_sem, xr_sem):
    r = lax.axis_index("rows")
    g = lax.axis_index("grp")
    m = r * 4 + g
    count = rows * 4
    has_nxt, has_prv = m < count - 1, m > 0
    has_up, has_down = r < rows - 1, r > 0
    inner = has_nxt & has_prv
    after = jnp.minimum(m + 1, count - 1)
    before = jnp.maximum(m - 1, 0)
    nxt = (after // 4, lax.rem(after, 4))
    prv = (before // 4, lax.rem(before, 4))
    up = (jnp.minimum(r + 1, rows - 1), g)
    down = (jnp.maximum(r - 1, 0), g)
    right = (r, lax.rem(g + 1, 4))
    left = (r, lax.rem(g + 3, 4))

    def when(there, act):
        if there is None:
            act()
        else:
            pl.when(there)(act)

    def remote(src, dst, ssem, rsem, dev):
        return pltpu.make_async_remote_copy(
            src_ref=src, dst_ref=dst, send_sem=ssem, recv_sem=rsem, device_id=dev, device_id_type=MESH)

    own = [pltpu.make_async_copy(cp.at[w], near.at[4 + w, pl.ds(0, 3)], own_sem.at[w]) for w in range(2)]
    own += [pltpu.make_async_copy(tf.at[w], near.at[4 + w, 3], own_sem.at[2 + w]) for w in range(2)]
    own += [pltpu.make_async_copy(res.at[:, pl.ds(B * e, B)], x3.at[4 + e], x_sem.at[e]) for e in range(8)]
    for copy in own:
        copy.start()

    def blank(side):
        trecv[side] = jnp.zeros_like(trecv[side])

    when(r == rows - 1, lambda: blank(0))
    when(r == 0, lambda: blank(1))
    barrier = pltpu.get_barrier_semaphore()
    for there, dev in ((has_nxt, nxt), (has_prv, prv), (has_up, up), (has_down, down), (None, right), (None, left)):
        when(there, lambda: pl.semaphore_signal(barrier, inc=1, device_id=dev, device_id_type=MESH))
    partners = 2
    for there in (has_nxt, has_prv, has_up, has_down):
        partners = partners + there.astype(jnp.int32)
    pl.semaphore_wait(barrier, partners)

    def source(w, t):
        return cp.at[w, t] if t < 3 else tf.at[w]

    sends = []

    def send(there, src, q, t, dev, lane):
        copy = remote(src, near.at[q, t], near_send.at[lane, t], near_recv.at[q, t], dev)
        when(there, copy.start)
        sends.append((there, copy))

    def arrived(there, q, t):
        when(there, remote(near.at[q, t], near.at[q, t], near_send.at[0, t], near_recv.at[q, t], nxt).wait_recv)

    for t in range(4):
        send(has_nxt, source(0, t), 2, t, nxt, 0)
        send(has_prv, source(1, t), 7, t, prv, 1)
    for t in range(4):
        send(has_nxt, source(1, t), 3, t, nxt, 2)
        send(has_prv, source(0, t), 6, t, prv, 3)
    halo = []
    for e in range(4):
        halo.append((has_up, has_down, remote(res.at[:, pl.ds(B * (4 + e), B)], x3.at[e], xr_sem.at[0, e], xr_sem.at[1, e], up)))
        halo.append((has_down, has_up, remote(res.at[:, pl.ds(B * e, B)], x3.at[12 + e], xr_sem.at[2, e], xr_sem.at[3, e], down)))
    for there, _, copy in halo:
        when(there, copy.start)
    for copy in own:
        copy.wait()
    middle = (g == 1) | (g == 2)
    first_slab, last_slab = middle & (r == 0), middle & (r == rows - 1)
    for t in range(4):
        arrived(has_prv, 2, t)
        send(inner, near.at[2, t], 0, t, nxt, 4)
        arrived(has_nxt, 7, t)
        send(inner, near.at[7, t], 9, t, prv, 5)
    for t in range(4):
        arrived(has_prv, 3, t)
        send(first_slab, near.at[3, t], 1, t, nxt, 8)
        arrived(has_nxt, 6, t)
        send(last_slab, near.at[6, t], 8, t, prv, 9)
    for t in range(4):
        arrived(m > 1, 0, t)
        send(has_down, near.at[0, t], 8, t, down, 6)
        arrived(m < count - 2, 9, t)
        send(has_up, near.at[9, t], 1, t, up, 7)
    for t in range(4):
        arrived(m < count - 2, 8, t)
        arrived(m > 1, 1, t)

    base = 2 * m - 4
    unit = eye()

    def picks(t):
        return order([nbr[k, t] for k in range(PAT)], NBR * r + t)

    def place(j):
        return jnp.clip(j - base, 0, 9)

    def diag(j):
        total = None
        for k in range(4):
            tile = near[place(j), k]
            part = dg(tile, tile, 1, 1)
            total = part if total is None else total + part
        return 2.0 * unit + total * (1.0 / B)

    def off(x, y):
        scale = jnp.where(linked(x, y), 1.0 / B, 0.0).astype(F32)
        return dg(near[place(x), tile_of(y - x)], near[place(y), tile_of(x - y)], 1, 1) * scale

    mine = [2 * g + w for w in range(2)]
    nodes = [picks(t)[0] for t in mine]
    ends = inverses([diag(nodes[w][k]) for w in range(2) for k in (0, 2)])
    held = []
    for w in range(2):
        i = NBR * r + mine[w]
        a, b, c = nodes[w]
        ia, ib, ic = split(off(i, a)), off(i, b), split(off(i, c))
        ab, cb = split(off(a, b)), split(off(c, b))
        inv_a, inv_c = split(ends[2 * w]), split(ends[2 * w + 1])
        za, zc = mm(ia, inv_a), mm(ic, inv_c)
        va, vc = split(mm(inv_a, ab)), split(mm(inv_c, cb))
        schur = diag(b) - mm(ab, va, 0, 0) - mm(cb, vc, 0, 0)
        rest_ib = ib - mm(ia, va) - mm(ic, vc)
        rest_ii = diag(i) - mm(split(za), ia, 1, 1) - mm(split(zc), ic, 1, 1)
        held.append((za, zc, va, vc, schur, rest_ib, rest_ii))
    mids = inverses([h[4] for h in held])
    tops = []
    for w in range(2):
        za, zc, va, vc, _, rest_ib, rest_ii = held[w]
        rs = split(rest_ib)
        yb = mm(rs, split(mids[w]))
        ys = split(yb)
        for k, y in enumerate((za - mm(ys, va, 1, 1), None, zc - mm(ys, vc, 1, 1))):
            yall[mine[w], k, 0], yall[mine[w], k, 1] = ys if y is None else split(y)
        tops.append(rest_ii - mm(ys, rs, 1, 1))

    def y_copy(t, k, dev, lane):
        return remote(yall.at[t, k], yall.at[t, k], y_send.at[lane, k], y_recv.at[t, k], dev)

    def u_copy(t, dev, lane):
        return remote(uall.at[t], uall.at[t], u_send.at[lane], u_recv.at[t], dev)

    from_left = 2 * lax.rem(g + 3, 4)
    from_right = 2 * lax.rem(g + 1, 4)
    across = 2 * lax.rem(g + 2, 4)
    y_sends = []
    for k in range(3):
        y_sends += [y_copy(mine[0], k, right, 0), y_copy(mine[1], k, left, 1)]
    for k in range(3):
        y_sends += [y_copy(mine[1], k, right, 2), y_copy(mine[0], k, left, 3)]
    for copy in y_sends:
        copy.start()

    upper = lax.broadcasted_iota(jnp.int32, (1, B), 1) >= HALF
    turned = [pltpu.roll(top, HALF, 1) for top in tops]
    corners = inverses([x[HALF:, :HALF] for x in turned])
    work, crosses = [], []
    for top, x, corner in zip(tops, turned, corners):
        cross = split(x[:HALF, :HALF])
        cross_s = mm(cross, split(corner))
        crosses.append(cross_s)
        rest = top[:HALF, :HALF] - mm(split(cross_s), cross, 1, 1)
        blank_half = jnp.zeros((HALF, HALF), F32)
        work.append(jnp.concatenate([blank_half, rest], axis=1))
        work.append(jnp.where(upper, top[HALF:, :], 0.0))
    swept = sweep(work)
    for w in range(2):
        head, foot = swept[2 * w][:, :HALF], swept[2 * w + 1]
        edge = mm(split(head), split(crosses[w]))
        uall[mine[w], 0:HALF, :] = jnp.concatenate([head, -edge], axis=1)
        uall[mine[w], HALF:HALF + HALF // 2, :] = jnp.concatenate(
            [foot[:HALF // 2, :HALF], foot[HALF // 2:, :HALF]], axis=1)
    for part in range(3):
        y_copy(from_left, part, right, 0).wait_recv()
        copy = y_copy(from_left, part, right, 4)
        copy.start()
        y_sends.append(copy)
        y_copy(from_right + 1, part, left, 0).wait_recv()
        copy = y_copy(from_right + 1, part, left, 5)
        copy.start()
        y_sends.append(copy)
    u_sends = [u_copy(mine[0], right, 0), u_copy(mine[1], left, 1), u_copy(mine[1], right, 2), u_copy(mine[0], left, 3)]
    for copy in u_sends:
        copy.start()

    acc[...] = jnp.zeros_like(acc)
    for there, back, copy in halo:
        when(there, copy.wait_send)
        when(back, copy.wait_recv)

    def y_of(t):
        return tuple(jnp.concatenate([yall[t, k, part] for k in range(3)], axis=1) for part in range(2))

    def gather(ts):
        seen = []
        for t in ts:
            ids, _, _ = picks(t)
            x = jnp.concatenate([x3[jnp.clip(j - (NBR * r - 4), 0, 15)] for j in ids], axis=1)
            seen.append((split(x), y_of(t), x3[4 + t]))
        return [own_x - mm(x, y, 1, 1) for x, y, own_x in seen]

    def factor(t):
        low = uall[t, HALF:HALF + HALF // 2, :]
        low = jnp.concatenate([pltpu.roll(low, HALF, 1), low], axis=0)
        return jnp.concatenate([uall[t, 0:HALF, :], jnp.where(upper, low, 0.0)], axis=0)

    def spread(ts, vs):
        us = [split(factor(t)) for t in ts]
        ws = [split(mm(split(v), u, 1, 1)) for v, u in zip(vs, us)]
        ws = [mm(w, u) for w, u in zip(ws, us)]
        terms = [mm(split(w), y_of(t)) for w, t in zip(ws, ts)]
        for t, w, term in zip(ts, ws, terms):
            ids, _, _ = picks(t)
            acc[4 + t] += w
            for gap in REACH:
                part = None
                for k in range(3):
                    weight = jnp.where(ids[k] == NBR * r + t + gap, 1.0, 0.0).astype(F32)
                    piece = term[:, B * k:B * k + B] * weight
                    part = piece if part is None else part + piece
                acc[4 + t + gap] -= part

    vs = gather(mine)
    u_copy(from_left, right, 0).wait_recv()
    copy = u_copy(from_left, right, 4)
    copy.start()
    u_sends.append(copy)
    u_copy(from_right + 1, left, 0).wait_recv()
    copy = u_copy(from_right + 1, left, 5)
    copy.start()
    u_sends.append(copy)
    spread(mine, vs)
    others = [from_left, from_right + 1, from_left + 1, from_right]
    for t in others[2:]:
        for k in range(3):
            y_copy(t, k, right, 0).wait_recv()
        u_copy(t, right, 0).wait_recv()
    spread(others, gather(others))
    last = [across, across + 1]
    for t in last:
        for k in range(3):
            y_copy(t, k, right, 0).wait_recv()
    vs = gather(last)
    for t in last:
        u_copy(t, right, 0).wait_recv()
    spread(last, vs)

    for e in range(4):
        tsend[0, e] = acc[e].astype(BF)
        tsend[1, e] = acc[12 + e].astype(BF)
    swaps = [(has_down, has_up, remote(tsend.at[0], trecv.at[0], t_sem.at[0], t_sem.at[1], down)),
             (has_up, has_down, remote(tsend.at[1], trecv.at[1], t_sem.at[2], t_sem.at[3], up))]
    for there, _, copy in swaps:
        when(there, copy.start)

    for w in range(2):
        t = 0
        for k in range(NBR):
            t = t + jnp.where(slot[0, k] == 2 * g + w, k, 0)
        t = jnp.minimum(t, NBR - 1)
        _, pos, s = picks(t)
        u = factor(t)
        us = split(u)
        for a in range(PAT):
            k = jnp.where(pos[1] == a, 1, jnp.where(pos[2] == a, 2, 0))
            self_ = (s == a).astype(F32)
            out_f[w, :, B * a:B * a + B] = u * self_ - mm(us, (yall[t, k, 0], yall[t, k, 1])) * (1.0 - self_)

    for there, back, copy in swaps:
        when(there, copy.wait_send)
        when(back, copy.wait_recv)
    for e in range(4):
        out_x[:, B * e:B * e + B] = acc[4 + e] + trecv[1, e].astype(F32)
        out_x[:, B * (4 + e):B * (4 + e) + B] = acc[8 + e] + trecv[0, e].astype(F32)
    for there, copy in sends:
        when(there, copy.wait_send)
    for copy in y_sends + u_sends:
        copy.wait_send()


def solution(mesh):
    rows = mesh.shape["rows"]
    smem = pl.BlockSpec(memory_space=pltpu.SMEM)
    raw = pl.BlockSpec(memory_space=pltpu.HBM)
    whole = pl.BlockSpec(memory_space=pltpu.VMEM)

    def local(tile_factor, coupling, nbr_list, setup_slot, residual):
        columns = residual.shape[0]
        dma = pltpu.SemaphoreType.DMA
        factor, result = pl.pallas_call(
            functools.partial(kernel, rows),
            out_shape=(
                jax.ShapeDtypeStruct((2, B, PAT * B), F32),
                jax.ShapeDtypeStruct((columns, NBR * B), F32),
            ),
            in_specs=[smem, smem, raw, raw, raw],
            out_specs=(whole, whole),
            scratch_shapes=[
                pltpu.VMEM((10, 4, B, B), BF),
                pltpu.VMEM((NBR, 3, 2, B, B), BF),
                pltpu.VMEM((NBR, HALF + HALF // 2, B), F32),
                pltpu.VMEM((16, columns, B), F32),
                pltpu.VMEM((16, columns, B), F32),
                pltpu.VMEM((2, 4, columns, B), BF),
                pltpu.VMEM((2, 4, columns, B), BF),
                dma((4,)), dma((8,)), dma((10, 4)), dma((10, 4)), dma((6, 3)), dma((NBR, 3)),
                dma((6,)), dma((NBR,)), dma((4,)), dma((4, 4)),
            ],
            compiler_params=pltpu.CompilerParams(
                collective_id=0, has_side_effects=True, vmem_limit_bytes=67043328
            ),
        )(nbr_list.T, setup_slot, tile_factor, coupling, residual)
        return factor, result

    return jax.shard_map(
        local,
        mesh=mesh,
        in_specs=(
            P(("rows", "grp"), None, None),
            P(("rows", "grp"), None, None, None),
            P("rows", None),
            P("rows", None),
            P("grp", "rows"),
        ),
        out_specs=(P(("rows", "grp"), None, None), P("grp", "rows")),
        check_vma=False,
    )
```

```python
import functools

import jax
import jax.numpy as jnp
from jax import lax
from jax.experimental import pallas as pl
from jax.experimental.pallas import tpu as pltpu
from jax.sharding import PartitionSpec as P

F32 = jnp.float32
BF = jnp.bfloat16
MESH = pl.DeviceIdType.MESH
B = 128
PAT = 4
NBR = 8
REACH = (-4, -3, -1, 1, 3, 4)
DOUBLINGS = 8
HALF = 64


def split(x):
    high = x.astype(BF)
    return high, (x - high.astype(F32)).astype(BF)


def dg(a, b, ca, cb):
    return lax.dot_general(a, b, (((ca,), (cb,)), ((), ())), preferred_element_type=F32)


def mm(a, b, ca=1, cb=0):
    return dg(a[0], b[0], ca, cb) + (dg(a[0], b[1], ca, cb) + dg(a[1], b[0], ca, cb))


def eye(n=B):
    shape = (n, n)
    return (lax.broadcasted_iota(jnp.int32, shape, 0) == lax.broadcasted_iota(jnp.int32, shape, 1)).astype(F32)


def inverses(mats):
    size = mats[0].shape[0]
    unit = eye(size)
    start = []
    for mat in mats:
        norm = jnp.max(jnp.sum(jnp.abs(mat), axis=0, keepdims=True), axis=1, keepdims=True)
        scale = 2.0 / (2.0 + norm)
        start.append((unit - mat * scale, unit, 2.0 * scale, scale))

    def double(_, state):
        new = []
        for power, series, low, factor in state:
            ph, pl_ = split(power)
            sh, sl = split(series)
            gain = low * (2.0 - low)
            s = 2.0 / (1.0 + gain)
            if size == B:
                first = jnp.concatenate([ph, sh], axis=1)
                out = dg(jnp.concatenate([ph, pl_], axis=1), jnp.concatenate([first, first], axis=0), 1, 0)
                out = out + dg(ph, jnp.concatenate([pl_, sl], axis=1), 1, 0)
                square, step = out[:, :B], out[:, B:]
            else:
                square, step = mm((ph, pl_), (ph, pl_)), mm((ph, pl_), (sh, sl))
            new.append((square * s + unit * (1.0 - s), series + step, gain * s, factor * s))
        return tuple(new)

    state = lax.fori_loop(0, DOUBLINGS, double, tuple(start))
    result = []
    for mat, (_, series, _, factor) in zip(mats, state):
        guess = series * factor
        gs = split(guess)
        miss = unit - mm(split(mat), gs)
        result.append(guess + mm(gs, split(miss)))
    return result


def sweep(mats):
    lane = lax.broadcasted_iota(jnp.int32, (1, B), 1)
    sub = lax.broadcasted_iota(jnp.int32, (8, 1), 0)

    def round_(it, state):
        done = []
        for mat in state:
            mat = list(mat)
            live = [(it <= p).astype(F32) for p in range(7)]
            for s in range(7, -1, -1):
                at = 120 + s
                row = mat[7][s:s + 1, :]
                pivot = row[:, at:at + 1]
                inv = 1.0 / pivot
                scaled = jnp.where(lane == at, 1.0 + inv, row * inv)
                for p in range(8):
                    c = mat[p][:, at:at + 1]
                    if p == 7:
                        if s == 0:
                            continue
                        c = jnp.where(sub < s, c, 0.0)
                    else:
                        c = c * live[p]
                    mat[p] = mat[p] - c * scaled
                final = jnp.where((lane >= 8 * it) & (lane < at), 0.0, jnp.where(lane == at, 1.0, row)) * lax.rsqrt(pivot)
                mat[7] = jnp.where(sub == s, final, mat[7])
            mat = [pltpu.roll(x, 8, 1) for x in mat]
            done.append(tuple([mat[7]] + mat[:7]))
        return tuple(done)

    slabs = lax.fori_loop(0, 8, round_, tuple(tuple(x[8 * p:8 * p + 8, :] for p in range(8)) for x in mats))
    return [jnp.concatenate(x, axis=0) for x in slabs]


def linked(x, y):
    gap = jnp.abs(x - y)
    return (gap == 1) | (gap == 3) | (gap == 4)


def tile_of(gap):
    return jnp.where(gap == 1, 1, jnp.where((gap == 3) | (gap == 4), 2, jnp.where(gap == -3, 1, 0)))


def order(p, i):
    s = jnp.where(p[0] == i, 0, jnp.where(p[1] == i, 1, jnp.where(p[2] == i, 2, 3)))
    pos = [jnp.where(s <= k, k + 1, k) for k in range(3)]
    nb = [jnp.where(s <= k, p[k + 1], p[k]) for k in range(3)]
    mid = jnp.where(linked(nb[1], nb[2]), jnp.where(linked(nb[0], nb[2]), 2, 1), 0)

    def three(v):
        b = jnp.where(mid == 0, v[0], jnp.where(mid == 1, v[1], v[2]))
        return jnp.where(mid == 0, v[1], v[0]), b, jnp.where(mid == 2, v[1], v[2])

    return three(nb), three(pos), s


def kernel(rows, nbr, slot, tf, cp, res, out_f, out_x, near, yall, uall, x3, acc, tsend, trecv, dbuf,
           own_sem, x_sem, near_send, near_recv, y_send, y_recv, u_send, u_recv, t_sem, xr_sem):
    r = lax.axis_index("rows")
    g = lax.axis_index("grp")
    m = r * 4 + g
    count = rows * 4
    has_nxt, has_prv = m < count - 1, m > 0
    has_up, has_down = r < rows - 1, r > 0
    inner = has_nxt & has_prv
    after = jnp.minimum(m + 1, count - 1)
    before = jnp.maximum(m - 1, 0)
    nxt = (after // 4, lax.rem(after, 4))
    prv = (before // 4, lax.rem(before, 4))
    up = (jnp.minimum(r + 1, rows - 1), g)
    down = (jnp.maximum(r - 1, 0), g)
    right = (r, lax.rem(g + 1, 4))
    left = (r, lax.rem(g + 3, 4))

    def when(there, act):
        if there is None:
            act()
        else:
            pl.when(there)(act)

    def remote(src, dst, ssem, rsem, dev):
        return pltpu.make_async_remote_copy(
            src_ref=src, dst_ref=dst, send_sem=ssem, recv_sem=rsem, device_id=dev, device_id_type=MESH)

    own = [pltpu.make_async_copy(cp.at[w], near.at[4 + w, pl.ds(0, 3)], own_sem.at[w]) for w in range(2)]
    own += [pltpu.make_async_copy(tf.at[w], near.at[4 + w, 3], own_sem.at[2 + w]) for w in range(2)]
    own += [pltpu.make_async_copy(res.at[:, pl.ds(B * e, B)], x3.at[4 + e], x_sem.at[e]) for e in range(8)]
    for copy in own:
        copy.start()

    def blank(side):
        trecv[side] = jnp.zeros_like(trecv[side])

    when(r == rows - 1, lambda: blank(0))
    when(r == 0, lambda: blank(1))
    barrier = pltpu.get_barrier_semaphore()
    for there, dev in ((has_nxt, nxt), (has_prv, prv), (has_up, up), (has_down, down), (None, right), (None, left)):
        when(there, lambda: pl.semaphore_signal(barrier, inc=1, device_id=dev, device_id_type=MESH))
    partners = 2
    for there in (has_nxt, has_prv, has_up, has_down):
        partners = partners + there.astype(jnp.int32)
    pl.semaphore_wait(barrier, partners)

    def source(w, t):
        return cp.at[w, t] if t < 3 else tf.at[w]

    sends = []

    def send(there, src, q, t, dev, lane):
        copy = remote(src, near.at[q, t], near_send.at[lane, t], near_recv.at[q, t], dev)
        when(there, copy.start)
        sends.append((there, copy))

    def arrived(there, q, t):
        when(there, remote(near.at[q, t], near.at[q, t], near_send.at[0, t], near_recv.at[q, t], nxt).wait_recv)

    for t in range(4):
        send(has_nxt, source(0, t), 2, t, nxt, 0)
        send(has_prv, source(1, t), 7, t, prv, 1)
    for t in range(4):
        send(has_nxt, source(1, t), 3, t, nxt, 2)
        send(has_prv, source(0, t), 6, t, prv, 3)
    halo = []
    for e in range(4):
        halo.append((has_up, has_down, remote(res.at[:, pl.ds(B * (4 + e), B)], x3.at[e], xr_sem.at[0, e], xr_sem.at[1, e], up)))
        halo.append((has_down, has_up, remote(res.at[:, pl.ds(B * e, B)], x3.at[12 + e], xr_sem.at[2, e], xr_sem.at[3, e], down)))
    for there, _, copy in halo:
        when(there, copy.start)
    for copy in own:
        copy.wait()
    unit = eye()

    def form(q):
        total = None
        for k in range(4):
            tile = near[q, k]
            part = dg(tile, tile, 1, 1)
            total = part if total is None else total + part
        dbuf[q] = 2.0 * unit + total * (1.0 / B)

    middle = (g == 1) | (g == 2)
    first_slab, last_slab = middle & (r == 0), middle & (r == rows - 1)
    for t in range(4):
        arrived(has_prv, 2, t)
        send(inner, near.at[2, t], 0, t, nxt, 4)
        arrived(has_nxt, 7, t)
        send(inner, near.at[7, t], 9, t, prv, 5)
    form(4)
    form(5)
    for t in range(4):
        arrived(has_prv, 3, t)
        send(first_slab, near.at[3, t], 1, t, nxt, 8)
        arrived(has_nxt, 6, t)
        send(last_slab, near.at[6, t], 8, t, prv, 9)
    form(2)
    form(7)
    for t in range(4):
        arrived(m > 1, 0, t)
        send(has_down, near.at[0, t], 8, t, down, 6)
        arrived(m < count - 2, 9, t)
        send(has_up, near.at[9, t], 1, t, up, 7)
    for q in (3, 6, 0, 9):
        form(q)
    for t in range(4):
        arrived(m < count - 2, 8, t)
        arrived(m > 1, 1, t)
    form(8)
    form(1)

    base = 2 * m - 4

    def picks(t):
        return order([nbr[k, t] for k in range(PAT)], NBR * r + t)

    def place(j):
        return jnp.clip(j - base, 0, 9)

    def diag(j):
        return dbuf[place(j)]

    def off(x, y):
        scale = jnp.where(linked(x, y), 1.0 / B, 0.0).astype(F32)
        return dg(near[place(x), tile_of(y - x)], near[place(y), tile_of(x - y)], 1, 1) * scale

    mine = [2 * g + w for w in range(2)]
    nodes = [picks(t)[0] for t in mine]
    ends = inverses([diag(nodes[w][k]) for w in range(2) for k in (0, 2)])
    held = []
    for w in range(2):
        i = NBR * r + mine[w]
        a, b, c = nodes[w]
        ia, ib, ic = split(off(i, a)), off(i, b), split(off(i, c))
        ab, cb = split(off(a, b)), split(off(c, b))
        inv_a, inv_c = split(ends[2 * w]), split(ends[2 * w + 1])
        za, zc = mm(ia, inv_a), mm(ic, inv_c)
        va, vc = split(mm(inv_a, ab)), split(mm(inv_c, cb))
        schur = diag(b) - mm(ab, va, 0, 0) - mm(cb, vc, 0, 0)
        rest_ib = ib - mm(ia, va) - mm(ic, vc)
        rest_ii = diag(i) - mm(split(za), ia, 1, 1) - mm(split(zc), ic, 1, 1)
        held.append((za, zc, va, vc, schur, rest_ib, rest_ii))
    mids = inverses([h[4] for h in held])
    tops = []
    for w in range(2):
        za, zc, va, vc, _, rest_ib, rest_ii = held[w]
        rs = split(rest_ib)
        yb = mm(rs, split(mids[w]))
        ys = split(yb)
        for k, y in enumerate((za - mm(ys, va, 1, 1), None, zc - mm(ys, vc, 1, 1))):
            yall[mine[w], k, 0], yall[mine[w], k, 1] = ys if y is None else split(y)
        tops.append(rest_ii - mm(ys, rs, 1, 1))

    def y_copy(t, k, dev, lane):
        return remote(yall.at[t, k], yall.at[t, k], y_send.at[lane, k], y_recv.at[t, k], dev)

    def u_copy(t, dev, lane):
        return remote(uall.at[t], uall.at[t], u_send.at[lane], u_recv.at[t], dev)

    from_left = 2 * lax.rem(g + 3, 4)
    from_right = 2 * lax.rem(g + 1, 4)
    across = 2 * lax.rem(g + 2, 4)
    y_sends = []
    for k in range(3):
        y_sends += [y_copy(mine[0], k, right, 0), y_copy(mine[1], k, left, 1)]
    for k in range(3):
        y_sends += [y_copy(mine[1], k, right, 2), y_copy(mine[0], k, left, 3)]
    for copy in y_sends:
        copy.start()

    upper = lax.broadcasted_iota(jnp.int32, (1, B), 1) >= HALF
    turned = [pltpu.roll(top, HALF, 1) for top in tops]
    corners = inverses([x[HALF:, :HALF] for x in turned])
    work, crosses = [], []
    for top, x, corner in zip(tops, turned, corners):
        cross = split(x[:HALF, :HALF])
        cross_s = mm(cross, split(corner))
        crosses.append(cross_s)
        rest = top[:HALF, :HALF] - mm(split(cross_s), cross, 1, 1)
        blank_half = jnp.zeros((HALF, HALF), F32)
        work.append(jnp.concatenate([blank_half, rest], axis=1))
        work.append(jnp.where(upper, top[HALF:, :], 0.0))
    swept = sweep(work)
    for w in range(2):
        head, foot = swept[2 * w][:, :HALF], swept[2 * w + 1]
        edge = mm(split(head), split(crosses[w]))
        uall[mine[w], 0:HALF, :] = jnp.concatenate([head, -edge], axis=1)
        uall[mine[w], HALF:HALF + HALF // 2, :] = jnp.concatenate(
            [foot[:HALF // 2, :HALF], foot[HALF // 2:, :HALF]], axis=1)
    for part in range(3):
        y_copy(from_left, part, right, 0).wait_recv()
        copy = y_copy(from_left, part, right, 4)
        copy.start()
        y_sends.append(copy)
        y_copy(from_right + 1, part, left, 0).wait_recv()
        copy = y_copy(from_right + 1, part, left, 5)
        copy.start()
        y_sends.append(copy)
    u_sends = [u_copy(mine[0], right, 0), u_copy(mine[1], left, 1), u_copy(mine[1], right, 2), u_copy(mine[0], left, 3)]
    for copy in u_sends:
        copy.start()

    acc[...] = jnp.zeros_like(acc)
    for there, back, copy in halo:
        when(there, copy.wait_send)
        when(back, copy.wait_recv)

    def y_of(t):
        return tuple(jnp.concatenate([yall[t, k, part] for k in range(3)], axis=1) for part in range(2))

    def gather(ts):
        seen = []
        for t in ts:
            ids, _, _ = picks(t)
            x = jnp.concatenate([x3[jnp.clip(j - (NBR * r - 4), 0, 15)] for j in ids], axis=1)
            seen.append((split(x), y_of(t), x3[4 + t]))
        return [own_x - mm(x, y, 1, 1) for x, y, own_x in seen]

    def factor(t):
        low = uall[t, HALF:HALF + HALF // 2, :]
        low = jnp.concatenate([pltpu.roll(low, HALF, 1), low], axis=0)
        return jnp.concatenate([uall[t, 0:HALF, :], jnp.where(upper, low, 0.0)], axis=0)

    def spread(ts, vs):
        us = [split(factor(t)) for t in ts]
        ws = [split(mm(split(v), u, 1, 1)) for v, u in zip(vs, us)]
        ws = [mm(w, u) for w, u in zip(ws, us)]
        terms = [mm(split(w), y_of(t)) for w, t in zip(ws, ts)]
        for t, w, term in zip(ts, ws, terms):
            ids, _, _ = picks(t)
            acc[4 + t] += w
            for gap in REACH:
                part = None
                for k in range(3):
                    weight = jnp.where(ids[k] == NBR * r + t + gap, 1.0, 0.0).astype(F32)
                    piece = term[:, B * k:B * k + B] * weight
                    part = piece if part is None else part + piece
                acc[4 + t + gap] -= part

    vs = gather(mine)
    u_copy(from_left, right, 0).wait_recv()
    copy = u_copy(from_left, right, 4)
    copy.start()
    u_sends.append(copy)
    u_copy(from_right + 1, left, 0).wait_recv()
    copy = u_copy(from_right + 1, left, 5)
    copy.start()
    u_sends.append(copy)
    spread(mine, vs)
    others = [from_left, from_right + 1, from_left + 1, from_right]
    for t in others[2:]:
        for k in range(3):
            y_copy(t, k, right, 0).wait_recv()
        u_copy(t, right, 0).wait_recv()
    spread(others, gather(others))
    last = [across, across + 1]
    for t in last:
        for k in range(3):
            y_copy(t, k, right, 0).wait_recv()
    vs = gather(last)
    for t in last:
        u_copy(t, right, 0).wait_recv()
    spread(last, vs)

    for e in range(4):
        tsend[0, e] = acc[e].astype(BF)
        tsend[1, e] = acc[12 + e].astype(BF)
    swaps = [(has_down, has_up, remote(tsend.at[0], trecv.at[0], t_sem.at[0], t_sem.at[1], down)),
             (has_up, has_down, remote(tsend.at[1], trecv.at[1], t_sem.at[2], t_sem.at[3], up))]
    for there, _, copy in swaps:
        when(there, copy.start)

    for w in range(2):
        t = 0
        for k in range(NBR):
            t = t + jnp.where(slot[0, k] == 2 * g + w, k, 0)
        t = jnp.minimum(t, NBR - 1)
        _, pos, s = picks(t)
        u = factor(t)
        us = split(u)
        for a in range(PAT):
            k = jnp.where(pos[1] == a, 1, jnp.where(pos[2] == a, 2, 0))
            self_ = (s == a).astype(F32)
            out_f[w, :, B * a:B * a + B] = u * self_ - mm(us, (yall[t, k, 0], yall[t, k, 1])) * (1.0 - self_)

    for there, back, copy in swaps:
        when(there, copy.wait_send)
        when(back, copy.wait_recv)
    for e in range(4):
        out_x[:, B * e:B * e + B] = acc[4 + e] + trecv[1, e].astype(F32)
        out_x[:, B * (4 + e):B * (4 + e) + B] = acc[8 + e] + trecv[0, e].astype(F32)
    for there, copy in sends:
        when(there, copy.wait_send)
    for copy in y_sends + u_sends:
        copy.wait_send()


def hand_on(factor, result, out_f, out_x):
    out_f[...] = factor[...]
    out_x[...] = result[...]


def solution(mesh):
    rows = mesh.shape["rows"]
    smem = pl.BlockSpec(memory_space=pltpu.SMEM)
    raw = pl.BlockSpec(memory_space=pltpu.HBM)
    whole = pl.BlockSpec(memory_space=pltpu.VMEM)

    def local(tile_factor, coupling, nbr_list, setup_slot, residual):
        columns = residual.shape[0]
        dma = pltpu.SemaphoreType.DMA
        factor, result = pl.pallas_call(
            functools.partial(kernel, rows),
            out_shape=(
                jax.ShapeDtypeStruct((2, B, PAT * B), F32),
                jax.ShapeDtypeStruct((columns, NBR * B), F32),
            ),
            in_specs=[smem, smem, raw, raw, raw],
            out_specs=(whole, whole),
            scratch_shapes=[
                pltpu.VMEM((10, 4, B, B), BF),
                pltpu.VMEM((NBR, 3, 2, B, B), BF),
                pltpu.VMEM((NBR, HALF + HALF // 2, B), F32),
                pltpu.VMEM((16, columns, B), F32),
                pltpu.VMEM((16, columns, B), F32),
                pltpu.VMEM((2, 4, columns, B), BF),
                pltpu.VMEM((2, 4, columns, B), BF),
                pltpu.VMEM((10, B, B), F32),
                dma((4,)), dma((8,)), dma((10, 4)), dma((10, 4)), dma((6, 3)), dma((NBR, 3)),
                dma((6,)), dma((NBR,)), dma((4,)), dma((4, 4)),
            ],
            compiler_params=pltpu.CompilerParams(
                collective_id=0, has_side_effects=True, vmem_limit_bytes=67043328
            ),
        )(nbr_list.T, setup_slot, tile_factor, coupling, residual)
        return pl.pallas_call(
            hand_on,
            out_shape=(jax.ShapeDtypeStruct(factor.shape, F32), jax.ShapeDtypeStruct(result.shape, F32)),
            in_specs=[whole, whole],
            out_specs=(whole, whole),
        )(factor, result)

    return jax.shard_map(
        local,
        mesh=mesh,
        in_specs=(
            P(("rows", "grp"), None, None),
            P(("rows", "grp"), None, None, None),
            P("rows", None),
            P("rows", None),
            P("grp", "rows"),
        ),
        out_specs=(P(("rows", "grp"), None, None), P("grp", "rows")),
        check_vma=False,
    )
```

```python
import functools

import jax
import jax.numpy as jnp
from jax import lax
from jax.experimental import pallas as pl
from jax.experimental.pallas import tpu as pltpu
from jax.sharding import PartitionSpec as P

F32 = jnp.float32
BF = jnp.bfloat16
MESH = pl.DeviceIdType.MESH
B = 128
PAT = 4
NBR = 8
REACH = (-4, -3, -1, 1, 3, 4)
DOUBLINGS = 8
HALF = 64


def split(x):
    high = x.astype(BF)
    return high, (x - high.astype(F32)).astype(BF)


def dg(a, b, ca, cb):
    return lax.dot_general(a, b, (((ca,), (cb,)), ((), ())), preferred_element_type=F32)


def mm(a, b, ca=1, cb=0):
    return dg(a[0], b[0], ca, cb) + (dg(a[0], b[1], ca, cb) + dg(a[1], b[0], ca, cb))


def eye(n=B):
    shape = (n, n)
    return (lax.broadcasted_iota(jnp.int32, shape, 0) == lax.broadcasted_iota(jnp.int32, shape, 1)).astype(F32)


def inverses(mats):
    size = mats[0].shape[0]
    unit = eye(size)
    start = []
    for mat in mats:
        norm = jnp.max(jnp.sum(jnp.abs(mat), axis=0, keepdims=True), axis=1, keepdims=True)
        scale = 2.0 / (2.0 + norm)
        start.append((unit - mat * scale, unit, 2.0 * scale, scale))

    def double(_, state):
        new = []
        for power, series, low, factor in state:
            ph, pl_ = split(power)
            sh, sl = split(series)
            gain = low * (2.0 - low)
            s = 2.0 / (1.0 + gain)
            if size == B:
                first = jnp.concatenate([ph, sh], axis=1)
                out = dg(jnp.concatenate([ph, pl_], axis=1), jnp.concatenate([first, first], axis=0), 1, 0)
                out = out + dg(ph, jnp.concatenate([pl_, sl], axis=1), 1, 0)
                square, step = out[:, :B], out[:, B:]
            else:
                square, step = mm((ph, pl_), (ph, pl_)), mm((ph, pl_), (sh, sl))
            new.append((square * s + unit * (1.0 - s), series + step, gain * s, factor * s))
        return tuple(new)

    state = lax.fori_loop(0, DOUBLINGS, double, tuple(start))
    result = []
    for mat, (_, series, _, factor) in zip(mats, state):
        guess = series * factor
        gs = split(guess)
        miss = unit - mm(split(mat), gs)
        result.append(guess + mm(gs, split(miss)))
    return result


def sweep(mats):
    lane = lax.broadcasted_iota(jnp.int32, (1, B), 1)
    sub = lax.broadcasted_iota(jnp.int32, (8, 1), 0)
    work = [[x[8 * p:8 * p + 8, :] for p in range(8)] for x in mats]
    for k in range(HALF - 1, -1, -1):
        top, s = divmod(k, 8)
        at = HALF + k
        for mat in work:
            row = mat[top][s:s + 1, :]
            pivot = row[:, at:at + 1]
            inv = 1.0 / pivot
            scaled = jnp.where(lane == at, 1.0 + inv, row * inv)
            for p in range(top + (s > 0)):
                c = mat[p][:, at:at + 1]
                if p == top:
                    c = jnp.where(sub < s, c, 0.0)
                mat[p] = mat[p] - c * scaled
            final = jnp.where(lane < at, 0.0, jnp.where(lane == at, 1.0, row)) * lax.rsqrt(pivot)
            mat[top] = jnp.where(sub == s, final, mat[top])
    return [pltpu.roll(jnp.concatenate(x, axis=0), HALF, 1) for x in work]


def linked(x, y):
    gap = jnp.abs(x - y)
    return (gap == 1) | (gap == 3) | (gap == 4)


def tile_of(gap):
    return jnp.where(gap == 1, 1, jnp.where((gap == 3) | (gap == 4), 2, jnp.where(gap == -3, 1, 0)))


def order(p, i):
    s = jnp.where(p[0] == i, 0, jnp.where(p[1] == i, 1, jnp.where(p[2] == i, 2, 3)))
    pos = [jnp.where(s <= k, k + 1, k) for k in range(3)]
    nb = [jnp.where(s <= k, p[k + 1], p[k]) for k in range(3)]
    mid = jnp.where(linked(nb[1], nb[2]), jnp.where(linked(nb[0], nb[2]), 2, 1), 0)

    def three(v):
        b = jnp.where(mid == 0, v[0], jnp.where(mid == 1, v[1], v[2]))
        return jnp.where(mid == 0, v[1], v[0]), b, jnp.where(mid == 2, v[1], v[2])

    return three(nb), three(pos), s


def kernel(rows, nbr, slot, tf, cp, res, out_f, out_x, near, yall, uall, x3, acc, tsend, trecv, dbuf,
           own_sem, x_sem, near_send, near_recv, y_send, y_recv, u_send, u_recv, t_sem, xr_sem):
    r = lax.axis_index("rows")
    g = lax.axis_index("grp")
    m = r * 4 + g
    count = rows * 4
    has_nxt, has_prv = m < count - 1, m > 0
    has_up, has_down = r < rows - 1, r > 0
    inner = has_nxt & has_prv
    after = jnp.minimum(m + 1, count - 1)
    before = jnp.maximum(m - 1, 0)
    nxt = (after // 4, lax.rem(after, 4))
    prv = (before // 4, lax.rem(before, 4))
    up = (jnp.minimum(r + 1, rows - 1), g)
    down = (jnp.maximum(r - 1, 0), g)
    right = (r, lax.rem(g + 1, 4))
    left = (r, lax.rem(g + 3, 4))

    def when(there, act):
        if there is None:
            act()
        else:
            pl.when(there)(act)

    def remote(src, dst, ssem, rsem, dev):
        return pltpu.make_async_remote_copy(
            src_ref=src, dst_ref=dst, send_sem=ssem, recv_sem=rsem, device_id=dev, device_id_type=MESH)

    own = [pltpu.make_async_copy(cp.at[w], near.at[4 + w, pl.ds(0, 3)], own_sem.at[w]) for w in range(2)]
    own += [pltpu.make_async_copy(tf.at[w], near.at[4 + w, 3], own_sem.at[2 + w]) for w in range(2)]
    own += [pltpu.make_async_copy(res.at[:, pl.ds(B * e, B)], x3.at[4 + e], x_sem.at[e]) for e in range(8)]
    for copy in own:
        copy.start()

    def blank(side):
        trecv[side] = jnp.zeros_like(trecv[side])

    when(r == rows - 1, lambda: blank(0))
    when(r == 0, lambda: blank(1))
    barrier = pltpu.get_barrier_semaphore()
    for there, dev in ((has_nxt, nxt), (has_prv, prv), (has_up, up), (has_down, down), (None, right), (None, left)):
        when(there, lambda: pl.semaphore_signal(barrier, inc=1, device_id=dev, device_id_type=MESH))
    partners = 2
    for there in (has_nxt, has_prv, has_up, has_down):
        partners = partners + there.astype(jnp.int32)
    pl.semaphore_wait(barrier, partners)

    def source(w, t):
        return cp.at[w, t] if t < 3 else tf.at[w]

    sends = []

    def send(there, src, q, t, dev, lane):
        copy = remote(src, near.at[q, t], near_send.at[lane, t], near_recv.at[q, t], dev)
        when(there, copy.start)
        sends.append((there, copy))

    def arrived(there, q, t):
        when(there, remote(near.at[q, t], near.at[q, t], near_send.at[0, t], near_recv.at[q, t], nxt).wait_recv)

    for t in range(4):
        send(has_nxt, source(0, t), 2, t, nxt, 0)
        send(has_prv, source(1, t), 7, t, prv, 1)
    for t in range(4):
        send(has_nxt, source(1, t), 3, t, nxt, 2)
        send(has_prv, source(0, t), 6, t, prv, 3)
    halo = []
    for e in range(4):
        halo.append((has_up, has_down, remote(res.at[:, pl.ds(B * (4 + e), B)], x3.at[e], xr_sem.at[0, e], xr_sem.at[1, e], up)))
        halo.append((has_down, has_up, remote(res.at[:, pl.ds(B * e, B)], x3.at[12 + e], xr_sem.at[2, e], xr_sem.at[3, e], down)))
    for there, _, copy in halo:
        when(there, copy.start)
    for copy in own:
        copy.wait()
    unit = eye()

    def form(q):
        total = None
        for k in range(4):
            tile = near[q, k]
            part = dg(tile, tile, 1, 1)
            total = part if total is None else total + part
        dbuf[q] = 2.0 * unit + total * (1.0 / B)

    middle = (g == 1) | (g == 2)
    first_slab, last_slab = middle & (r == 0), middle & (r == rows - 1)
    for t in range(4):
        arrived(has_prv, 2, t)
        send(inner, near.at[2, t], 0, t, nxt, 4)
        arrived(has_nxt, 7, t)
        send(inner, near.at[7, t], 9, t, prv, 5)
    form(4)
    form(5)
    for t in range(4):
        arrived(has_prv, 3, t)
        send(first_slab, near.at[3, t], 1, t, nxt, 8)
        arrived(has_nxt, 6, t)
        send(last_slab, near.at[6, t], 8, t, prv, 9)
    form(2)
    form(7)
    for t in range(4):
        arrived(m > 1, 0, t)
        send(has_down, near.at[0, t], 8, t, down, 6)
        arrived(m < count - 2, 9, t)
        send(has_up, near.at[9, t], 1, t, up, 7)
    for q in (3, 6, 0, 9):
        form(q)
    for t in range(4):
        arrived(m < count - 2, 8, t)
        arrived(m > 1, 1, t)
    form(8)
    form(1)

    base = 2 * m - 4

    def picks(t):
        return order([nbr[k, t] for k in range(PAT)], NBR * r + t)

    def place(j):
        return jnp.clip(j - base, 0, 9)

    def diag(j):
        return dbuf[place(j)]

    def off(x, y):
        scale = jnp.where(linked(x, y), 1.0 / B, 0.0).astype(F32)
        return dg(near[place(x), tile_of(y - x)], near[place(y), tile_of(x - y)], 1, 1) * scale

    mine = [2 * g + w for w in range(2)]
    nodes = [picks(t)[0] for t in mine]
    ends = inverses([diag(nodes[w][k]) for w in range(2) for k in (0, 2)])
    held = []
    for w in range(2):
        i = NBR * r + mine[w]
        a, b, c = nodes[w]
        ia, ib, ic = split(off(i, a)), off(i, b), split(off(i, c))
        ab, cb = split(off(a, b)), split(off(c, b))
        inv_a, inv_c = split(ends[2 * w]), split(ends[2 * w + 1])
        za, zc = mm(ia, inv_a), mm(ic, inv_c)
        va, vc = split(mm(inv_a, ab)), split(mm(inv_c, cb))
        schur = diag(b) - mm(ab, va, 0, 0) - mm(cb, vc, 0, 0)
        rest_ib = ib - mm(ia, va) - mm(ic, vc)
        rest_ii = diag(i) - mm(split(za), ia, 1, 1) - mm(split(zc), ic, 1, 1)
        held.append((za, zc, va, vc, schur, rest_ib, rest_ii))
    mids = inverses([h[4] for h in held])
    tops = []
    for w in range(2):
        za, zc, va, vc, _, rest_ib, rest_ii = held[w]
        rs = split(rest_ib)
        yb = mm(rs, split(mids[w]))
        ys = split(yb)
        for k, y in enumerate((za - mm(ys, va, 1, 1), None, zc - mm(ys, vc, 1, 1))):
            yall[mine[w], k, 0], yall[mine[w], k, 1] = ys if y is None else split(y)
        tops.append(rest_ii - mm(ys, rs, 1, 1))

    def y_copy(t, k, dev, lane):
        return remote(yall.at[t, k], yall.at[t, k], y_send.at[lane, k], y_recv.at[t, k], dev)

    def u_copy(t, dev, lane):
        return remote(uall.at[t], uall.at[t], u_send.at[lane], u_recv.at[t], dev)

    from_left = 2 * lax.rem(g + 3, 4)
    from_right = 2 * lax.rem(g + 1, 4)
    across = 2 * lax.rem(g + 2, 4)
    y_sends = []
    for k in range(3):
        y_sends += [y_copy(mine[0], k, right, 0), y_copy(mine[1], k, left, 1)]
    for k in range(3):
        y_sends += [y_copy(mine[1], k, right, 2), y_copy(mine[0], k, left, 3)]
    for copy in y_sends:
        copy.start()

    upper = lax.broadcasted_iota(jnp.int32, (1, B), 1) >= HALF
    turned = [pltpu.roll(top, HALF, 1) for top in tops]
    corners = inverses([x[HALF:, :HALF] for x in turned])
    work, crosses = [], []
    for top, x, corner in zip(tops, turned, corners):
        cross = split(x[:HALF, :HALF])
        cross_s = mm(cross, split(corner))
        crosses.append(cross_s)
        rest = top[:HALF, :HALF] - mm(split(cross_s), cross, 1, 1)
        blank_half = jnp.zeros((HALF, HALF), F32)
        work.append(jnp.concatenate([blank_half, rest], axis=1))
        work.append(jnp.where(upper, top[HALF:, :], 0.0))
    swept = sweep(work)
    for w in range(2):
        head, foot = swept[2 * w][:, :HALF], swept[2 * w + 1]
        edge = mm(split(head), split(crosses[w]))
        uall[mine[w], 0:HALF, :] = jnp.concatenate([head, -edge], axis=1)
        uall[mine[w], HALF:HALF + HALF // 2, :] = jnp.concatenate(
            [foot[:HALF // 2, :HALF], foot[HALF // 2:, :HALF]], axis=1)
    for part in range(3):
        y_copy(from_left, part, right, 0).wait_recv()
        copy = y_copy(from_left, part, right, 4)
        copy.start()
        y_sends.append(copy)
        y_copy(from_right + 1, part, left, 0).wait_recv()
        copy = y_copy(from_right + 1, part, left, 5)
        copy.start()
        y_sends.append(copy)
    u_sends = [u_copy(mine[0], right, 0), u_copy(mine[1], left, 1), u_copy(mine[1], right, 2), u_copy(mine[0], left, 3)]
    for copy in u_sends:
        copy.start()

    acc[...] = jnp.zeros_like(acc)
    for there, back, copy in halo:
        when(there, copy.wait_send)
        when(back, copy.wait_recv)

    def y_of(t):
        return tuple(jnp.concatenate([yall[t, k, part] for k in range(3)], axis=1) for part in range(2))

    def gather(ts):
        seen = []
        for t in ts:
            ids, _, _ = picks(t)
            x = jnp.concatenate([x3[jnp.clip(j - (NBR * r - 4), 0, 15)] for j in ids], axis=1)
            seen.append((split(x), y_of(t), x3[4 + t]))
        return [own_x - mm(x, y, 1, 1) for x, y, own_x in seen]

    def factor(t):
        low = uall[t, HALF:HALF + HALF // 2, :]
        low = jnp.concatenate([pltpu.roll(low, HALF, 1), low], axis=0)
        return jnp.concatenate([uall[t, 0:HALF, :], jnp.where(upper, low, 0.0)], axis=0)

    def spread(ts, vs):
        us = [split(factor(t)) for t in ts]
        ws = [split(mm(split(v), u, 1, 1)) for v, u in zip(vs, us)]
        ws = [mm(w, u) for w, u in zip(ws, us)]
        terms = [mm(split(w), y_of(t)) for w, t in zip(ws, ts)]
        for t, w, term in zip(ts, ws, terms):
            ids, _, _ = picks(t)
            acc[4 + t] += w
            for gap in REACH:
                part = None
                for k in range(3):
                    weight = jnp.where(ids[k] == NBR * r + t + gap, 1.0, 0.0).astype(F32)
                    piece = term[:, B * k:B * k + B] * weight
                    part = piece if part is None else part + piece
                acc[4 + t + gap] -= part

    vs = gather(mine)
    u_copy(from_left, right, 0).wait_recv()
    copy = u_copy(from_left, right, 4)
    copy.start()
    u_sends.append(copy)
    u_copy(from_right + 1, left, 0).wait_recv()
    copy = u_copy(from_right + 1, left, 5)
    copy.start()
    u_sends.append(copy)
    spread(mine, vs)
    others = [from_left, from_right + 1, from_left + 1, from_right]
    for t in others[2:]:
        for k in range(3):
            y_copy(t, k, right, 0).wait_recv()
        u_copy(t, right, 0).wait_recv()
    spread(others, gather(others))
    last = [across, across + 1]
    for t in last:
        for k in range(3):
            y_copy(t, k, right, 0).wait_recv()
    vs = gather(last)
    for t in last:
        u_copy(t, right, 0).wait_recv()
    spread(last, vs)

    for e in range(4):
        tsend[0, e] = acc[e].astype(BF)
        tsend[1, e] = acc[12 + e].astype(BF)
    swaps = [(has_down, has_up, remote(tsend.at[0], trecv.at[0], t_sem.at[0], t_sem.at[1], down)),
             (has_up, has_down, remote(tsend.at[1], trecv.at[1], t_sem.at[2], t_sem.at[3], up))]
    for there, _, copy in swaps:
        when(there, copy.start)

    for w in range(2):
        t = 0
        for k in range(NBR):
            t = t + jnp.where(slot[0, k] == 2 * g + w, k, 0)
        t = jnp.minimum(t, NBR - 1)
        _, pos, s = picks(t)
        u = factor(t)
        us = split(u)
        for a in range(PAT):
            k = jnp.where(pos[1] == a, 1, jnp.where(pos[2] == a, 2, 0))
            self_ = (s == a).astype(F32)
            out_f[w, :, B * a:B * a + B] = u * self_ - mm(us, (yall[t, k, 0], yall[t, k, 1])) * (1.0 - self_)

    for there, back, copy in swaps:
        when(there, copy.wait_send)
        when(back, copy.wait_recv)
    for e in range(4):
        out_x[:, B * e:B * e + B] = acc[4 + e] + trecv[1, e].astype(F32)
        out_x[:, B * (4 + e):B * (4 + e) + B] = acc[8 + e] + trecv[0, e].astype(F32)
    for there, copy in sends:
        when(there, copy.wait_send)
    for copy in y_sends + u_sends:
        copy.wait_send()


def hand_on(factor, result, out_f, out_x):
    out_f[...] = factor[...]
    out_x[...] = result[...]


def solution(mesh):
    rows = mesh.shape["rows"]
    smem = pl.BlockSpec(memory_space=pltpu.SMEM)
    raw = pl.BlockSpec(memory_space=pltpu.HBM)
    whole = pl.BlockSpec(memory_space=pltpu.VMEM)

    def local(tile_factor, coupling, nbr_list, setup_slot, residual):
        columns = residual.shape[0]
        dma = pltpu.SemaphoreType.DMA
        factor, result = pl.pallas_call(
            functools.partial(kernel, rows),
            out_shape=(
                jax.ShapeDtypeStruct((2, B, PAT * B), F32),
                jax.ShapeDtypeStruct((columns, NBR * B), F32),
            ),
            in_specs=[smem, smem, raw, raw, raw],
            out_specs=(whole, whole),
            scratch_shapes=[
                pltpu.VMEM((10, 4, B, B), BF),
                pltpu.VMEM((NBR, 3, 2, B, B), BF),
                pltpu.VMEM((NBR, HALF + HALF // 2, B), F32),
                pltpu.VMEM((16, columns, B), F32),
                pltpu.VMEM((16, columns, B), F32),
                pltpu.VMEM((2, 4, columns, B), BF),
                pltpu.VMEM((2, 4, columns, B), BF),
                pltpu.VMEM((10, B, B), F32),
                dma((4,)), dma((8,)), dma((10, 4)), dma((10, 4)), dma((6, 3)), dma((NBR, 3)),
                dma((6,)), dma((NBR,)), dma((4,)), dma((4, 4)),
            ],
            compiler_params=pltpu.CompilerParams(
                collective_id=0, has_side_effects=True, vmem_limit_bytes=67043328
            ),
        )(nbr_list.T, setup_slot, tile_factor, coupling, residual)
        return pl.pallas_call(
            hand_on,
            out_shape=(jax.ShapeDtypeStruct(factor.shape, F32), jax.ShapeDtypeStruct(result.shape, F32)),
            in_specs=[whole, whole],
            out_specs=(whole, whole),
        )(factor, result)

    return jax.shard_map(
        local,
        mesh=mesh,
        in_specs=(
            P(("rows", "grp"), None, None),
            P(("rows", "grp"), None, None, None),
            P("rows", None),
            P("rows", None),
            P("grp", "rows"),
        ),
        out_specs=(P(("rows", "grp"), None, None), P("grp", "rows")),
        check_vma=False,
    )
```

```python
import functools

import jax
import jax.numpy as jnp
from jax import lax
from jax.experimental import pallas as pl
from jax.experimental.pallas import tpu as pltpu
from jax.sharding import PartitionSpec as P

F32 = jnp.float32
BF = jnp.bfloat16
MESH = pl.DeviceIdType.MESH
B = 128
PAT = 4
NBR = 8
REACH = (-4, -3, -1, 1, 3, 4)
DOUBLINGS = 8
HALF = 64


def split(x):
    high = x.astype(BF)
    return high, (x - high.astype(F32)).astype(BF)


def dg(a, b, ca, cb):
    return lax.dot_general(a, b, (((ca,), (cb,)), ((), ())), preferred_element_type=F32)


def mm(a, b, ca=1, cb=0):
    return dg(a[0], b[0], ca, cb) + (dg(a[0], b[1], ca, cb) + dg(a[1], b[0], ca, cb))


def eye(n=B):
    shape = (n, n)
    return (lax.broadcasted_iota(jnp.int32, shape, 0) == lax.broadcasted_iota(jnp.int32, shape, 1)).astype(F32)


def inverses(mats):
    size = mats[0].shape[0]
    unit = eye(size)
    start = []
    for mat in mats:
        norm = jnp.max(jnp.sum(jnp.abs(mat), axis=0, keepdims=True), axis=1, keepdims=True)
        scale = 2.0 / (2.0 + norm)
        start.append((unit - mat * scale, unit, 2.0 * scale, scale))

    def double(_, state):
        new = []
        for power, series, low, factor in state:
            ph, pl_ = split(power)
            sh, sl = split(series)
            gain = low * (2.0 - low)
            s = 2.0 / (1.0 + gain)
            if size == B:
                first = jnp.concatenate([ph, sh], axis=1)
                out = dg(jnp.concatenate([ph, pl_], axis=1), jnp.concatenate([first, first], axis=0), 1, 0)
                out = out + dg(ph, jnp.concatenate([pl_, sl], axis=1), 1, 0)
                square, step = out[:, :B], out[:, B:]
            else:
                square, step = mm((ph, pl_), (ph, pl_)), mm((ph, pl_), (sh, sl))
            new.append((square * s + unit * (1.0 - s), series + step, gain * s, factor * s))
        return tuple(new)

    state = lax.fori_loop(0, DOUBLINGS, double, tuple(start))
    result = []
    for mat, (_, series, _, factor) in zip(mats, state):
        guess = series * factor
        gs = split(guess)
        miss = unit - mm(split(mat), gs)
        result.append(guess + mm(gs, split(miss)))
    return result


def sweep(mats):
    lane = lax.broadcasted_iota(jnp.int32, (1, B), 1)
    sub = lax.broadcasted_iota(jnp.int32, (8, 1), 0)
    work = [[x[8 * p:8 * p + 8, :] for p in range(8)] for x in mats]
    for k in range(HALF - 1, -1, -1):
        top, s = divmod(k, 8)
        at = HALF + k
        for mat in work:
            row = mat[top][s:s + 1, :]
            pivot = row[:, at:at + 1]
            inv = 1.0 / pivot
            scaled = jnp.where(lane == at, 1.0 + inv, row * inv)
            for p in range(top + (s > 0)):
                c = mat[p][:, at:at + 1]
                if p == top:
                    c = jnp.where(sub < s, c, 0.0)
                mat[p] = mat[p] - c * scaled
            final = jnp.where(lane < at, 0.0, jnp.where(lane == at, 1.0, row)) * lax.rsqrt(pivot)
            mat[top] = jnp.where(sub == s, final, mat[top])
    return [pltpu.roll(jnp.concatenate(x, axis=0), HALF, 1) for x in work]


def linked(x, y):
    gap = jnp.abs(x - y)
    return (gap == 1) | (gap == 3) | (gap == 4)


def tile_of(gap):
    return jnp.where(gap == 1, 1, jnp.where((gap == 3) | (gap == 4), 2, jnp.where(gap == -3, 1, 0)))


def order(p, i):
    s = jnp.where(p[0] == i, 0, jnp.where(p[1] == i, 1, jnp.where(p[2] == i, 2, 3)))
    pos = [jnp.where(s <= k, k + 1, k) for k in range(3)]
    nb = [jnp.where(s <= k, p[k + 1], p[k]) for k in range(3)]
    mid = jnp.where(linked(nb[1], nb[2]), jnp.where(linked(nb[0], nb[2]), 2, 1), 0)

    def three(v):
        b = jnp.where(mid == 0, v[0], jnp.where(mid == 1, v[1], v[2]))
        return jnp.where(mid == 0, v[1], v[0]), b, jnp.where(mid == 2, v[1], v[2])

    return three(nb), three(pos), s


def kernel(rows, nbr, slot, tf, cp, res, out_f, out_x, near, yall, uall, x3, acc, tsend, trecv, dbuf,
           own_sem, x_sem, near_send, near_recv, y_send, y_recv, u_send, u_recv, t_sem, xr_sem):
    r = lax.axis_index("rows")
    g = lax.axis_index("grp")
    m = r * 4 + g
    count = rows * 4
    has_nxt, has_prv = m < count - 1, m > 0
    has_up, has_down = r < rows - 1, r > 0
    inner = has_nxt & has_prv
    after = jnp.minimum(m + 1, count - 1)
    before = jnp.maximum(m - 1, 0)
    nxt = (after // 4, lax.rem(after, 4))
    prv = (before // 4, lax.rem(before, 4))
    up = (jnp.minimum(r + 1, rows - 1), g)
    down = (jnp.maximum(r - 1, 0), g)
    right = (r, lax.rem(g + 1, 4))
    left = (r, lax.rem(g + 3, 4))

    def when(there, act):
        if there is None:
            act()
        else:
            pl.when(there)(act)

    def remote(src, dst, ssem, rsem, dev):
        return pltpu.make_async_remote_copy(
            src_ref=src, dst_ref=dst, send_sem=ssem, recv_sem=rsem, device_id=dev, device_id_type=MESH)

    own = [pltpu.make_async_copy(cp.at[w], near.at[4 + w, pl.ds(0, 3)], own_sem.at[w]) for w in range(2)]
    own += [pltpu.make_async_copy(tf.at[w], near.at[4 + w, 3], own_sem.at[2 + w]) for w in range(2)]
    own += [pltpu.make_async_copy(res.at[:, pl.ds(B * e, B)], x3.at[4 + e], x_sem.at[e]) for e in range(8)]
    for copy in own:
        copy.start()

    def blank(side):
        trecv[side] = jnp.zeros_like(trecv[side])

    when(r == rows - 1, lambda: blank(0))
    when(r == 0, lambda: blank(1))
    barrier = pltpu.get_barrier_semaphore()
    for there, dev in ((has_nxt, nxt), (has_prv, prv), (has_up, up), (has_down, down), (None, right), (None, left)):
        when(there, lambda: pl.semaphore_signal(barrier, inc=1, device_id=dev, device_id_type=MESH))
    partners = 2
    for there in (has_nxt, has_prv, has_up, has_down):
        partners = partners + there.astype(jnp.int32)
    pl.semaphore_wait(barrier, partners)

    def source(w, t):
        return cp.at[w, t] if t < 3 else tf.at[w]

    sends = []

    def send(there, src, q, t, dev, lane):
        copy = remote(src, near.at[q, t], near_send.at[lane, t], near_recv.at[q, t], dev)
        when(there, copy.start)
        sends.append((there, copy))

    def arrived(there, q, t):
        when(there, remote(near.at[q, t], near.at[q, t], near_send.at[0, t], near_recv.at[q, t], nxt).wait_recv)

    for t in range(4):
        send(has_nxt, source(0, t), 2, t, nxt, 0)
        send(has_prv, source(1, t), 7, t, prv, 1)
    for t in range(4):
        send(has_nxt, source(1, t), 3, t, nxt, 2)
        send(has_prv, source(0, t), 6, t, prv, 3)
    halo = []
    for e in range(4):
        halo.append((has_up, has_down, remote(res.at[:, pl.ds(B * (4 + e), B)], x3.at[e], xr_sem.at[0, e], xr_sem.at[1, e], up)))
        halo.append((has_down, has_up, remote(res.at[:, pl.ds(B * e, B)], x3.at[12 + e], xr_sem.at[2, e], xr_sem.at[3, e], down)))
    for copy in own:
        copy.wait()
    unit = eye()

    def form(q):
        total = None
        for k in range(4):
            tile = near[q, k]
            part = dg(tile, tile, 1, 1)
            total = part if total is None else total + part
        dbuf[q] = 2.0 * unit + total * (1.0 / B)

    middle = (g == 1) | (g == 2)
    first_slab, last_slab = middle & (r == 0), middle & (r == rows - 1)
    for t in range(4):
        arrived(has_prv, 2, t)
        send(inner, near.at[2, t], 0, t, nxt, 4)
        arrived(has_nxt, 7, t)
        send(inner, near.at[7, t], 9, t, prv, 5)
    form(4)
    form(5)
    for t in range(4):
        arrived(has_prv, 3, t)
        send(first_slab, near.at[3, t], 1, t, nxt, 8)
        arrived(has_nxt, 6, t)
        send(last_slab, near.at[6, t], 8, t, prv, 9)
    form(2)
    form(7)
    for t in range(4):
        arrived(m > 1, 0, t)
        send(has_down, near.at[0, t], 8, t, down, 6)
        arrived(m < count - 2, 9, t)
        send(has_up, near.at[9, t], 1, t, up, 7)
    for there, _, copy in halo:
        when(there, copy.start)
    for q in (3, 6, 0, 9):
        form(q)
    for t in range(4):
        arrived(m < count - 2, 8, t)
        arrived(m > 1, 1, t)
    form(8)
    form(1)

    base = 2 * m - 4

    def picks(t):
        return order([nbr[k, t] for k in range(PAT)], NBR * r + t)

    def place(j):
        return jnp.clip(j - base, 0, 9)

    def diag(j):
        return dbuf[place(j)]

    def off(x, y):
        scale = jnp.where(linked(x, y), 1.0 / B, 0.0).astype(F32)
        return dg(near[place(x), tile_of(y - x)], near[place(y), tile_of(x - y)], 1, 1) * scale

    mine = [2 * g + w for w in range(2)]
    nodes = [picks(t)[0] for t in mine]
    ends = inverses([diag(nodes[w][k]) for w in range(2) for k in (0, 2)])
    held = []
    for w in range(2):
        i = NBR * r + mine[w]
        a, b, c = nodes[w]
        ia, ib, ic = split(off(i, a)), off(i, b), split(off(i, c))
        ab, cb = split(off(a, b)), split(off(c, b))
        inv_a, inv_c = split(ends[2 * w]), split(ends[2 * w + 1])
        za, zc = mm(ia, inv_a), mm(ic, inv_c)
        va, vc = split(mm(inv_a, ab)), split(mm(inv_c, cb))
        schur = diag(b) - mm(ab, va, 0, 0) - mm(cb, vc, 0, 0)
        rest_ib = ib - mm(ia, va) - mm(ic, vc)
        rest_ii = diag(i) - mm(split(za), ia, 1, 1) - mm(split(zc), ic, 1, 1)
        held.append((za, zc, va, vc, schur, rest_ib, rest_ii))
    mids = inverses([h[4] for h in held])
    tops = []
    for w in range(2):
        za, zc, va, vc, _, rest_ib, rest_ii = held[w]
        rs = split(rest_ib)
        yb = mm(rs, split(mids[w]))
        ys = split(yb)
        for k, y in enumerate((za - mm(ys, va, 1, 1), None, zc - mm(ys, vc, 1, 1))):
            yall[mine[w], k, 0], yall[mine[w], k, 1] = ys if y is None else split(y)
        tops.append(rest_ii - mm(ys, rs, 1, 1))

    def y_copy(t, k, dev, lane):
        return remote(yall.at[t, k], yall.at[t, k], y_send.at[lane, k], y_recv.at[t, k], dev)

    def u_copy(t, dev, lane):
        return remote(uall.at[t], uall.at[t], u_send.at[lane], u_recv.at[t], dev)

    from_left = 2 * lax.rem(g + 3, 4)
    from_right = 2 * lax.rem(g + 1, 4)
    across = 2 * lax.rem(g + 2, 4)
    y_sends = []
    for k in range(3):
        y_sends += [y_copy(mine[0], k, right, 0), y_copy(mine[1], k, left, 1)]
    for k in range(3):
        y_sends += [y_copy(mine[1], k, right, 2), y_copy(mine[0], k, left, 3)]
    for copy in y_sends:
        copy.start()

    upper = lax.broadcasted_iota(jnp.int32, (1, B), 1) >= HALF
    turned = [pltpu.roll(top, HALF, 1) for top in tops]
    corners = inverses([x[HALF:, :HALF] for x in turned])
    work, crosses = [], []
    for top, x, corner in zip(tops, turned, corners):
        cross = split(x[:HALF, :HALF])
        cross_s = mm(cross, split(corner))
        crosses.append(cross_s)
        rest = top[:HALF, :HALF] - mm(split(cross_s), cross, 1, 1)
        blank_half = jnp.zeros((HALF, HALF), F32)
        work.append(jnp.concatenate([blank_half, rest], axis=1))
        work.append(jnp.where(upper, top[HALF:, :], 0.0))
    swept = sweep(work)
    for w in range(2):
        head, foot = swept[2 * w][:, :HALF], swept[2 * w + 1]
        edge = mm(split(head), split(crosses[w]))
        uall[mine[w], 0:HALF, :] = jnp.concatenate([head, -edge], axis=1)
        uall[mine[w], HALF:HALF + HALF // 2, :] = jnp.concatenate(
            [foot[:HALF // 2, :HALF], foot[HALF // 2:, :HALF]], axis=1)
    for part in range(3):
        y_copy(from_left, part, right, 0).wait_recv()
        copy = y_copy(from_left, part, right, 4)
        copy.start()
        y_sends.append(copy)
        y_copy(from_right + 1, part, left, 0).wait_recv()
        copy = y_copy(from_right + 1, part, left, 5)
        copy.start()
        y_sends.append(copy)
    u_sends = [u_copy(mine[0], right, 0), u_copy(mine[1], left, 1), u_copy(mine[1], right, 2), u_copy(mine[0], left, 3)]
    for copy in u_sends:
        copy.start()

    acc[...] = jnp.zeros_like(acc)
    for there, back, copy in halo:
        when(there, copy.wait_send)
        when(back, copy.wait_recv)

    def y_of(t):
        return tuple(jnp.concatenate([yall[t, k, part] for k in range(3)], axis=1) for part in range(2))

    def gather(ts):
        seen = []
        for t in ts:
            ids, _, _ = picks(t)
            x = jnp.concatenate([x3[jnp.clip(j - (NBR * r - 4), 0, 15)] for j in ids], axis=1)
            seen.append((split(x), y_of(t), x3[4 + t]))
        return [own_x - mm(x, y, 1, 1) for x, y, own_x in seen]

    def factor(t):
        low = uall[t, HALF:HALF + HALF // 2, :]
        low = jnp.concatenate([pltpu.roll(low, HALF, 1), low], axis=0)
        return jnp.concatenate([uall[t, 0:HALF, :], jnp.where(upper, low, 0.0)], axis=0)

    def spread(ts, vs):
        us = [split(factor(t)) for t in ts]
        ws = [split(mm(split(v), u, 1, 1)) for v, u in zip(vs, us)]
        ws = [mm(w, u) for w, u in zip(ws, us)]
        terms = [mm(split(w), y_of(t)) for w, t in zip(ws, ts)]
        for t, w, term in zip(ts, ws, terms):
            ids, _, _ = picks(t)
            acc[4 + t] += w
            for gap in REACH:
                part = None
                for k in range(3):
                    weight = jnp.where(ids[k] == NBR * r + t + gap, 1.0, 0.0).astype(F32)
                    piece = term[:, B * k:B * k + B] * weight
                    part = piece if part is None else part + piece
                acc[4 + t + gap] -= part

    vs = gather(mine)
    u_copy(from_left, right, 0).wait_recv()
    copy = u_copy(from_left, right, 4)
    copy.start()
    u_sends.append(copy)
    u_copy(from_right + 1, left, 0).wait_recv()
    copy = u_copy(from_right + 1, left, 5)
    copy.start()
    u_sends.append(copy)
    spread(mine, vs)
    others = [from_left, from_right + 1, from_left + 1, from_right]
    for t in others[2:]:
        for k in range(3):
            y_copy(t, k, right, 0).wait_recv()
        u_copy(t, right, 0).wait_recv()
    spread(others, gather(others))
    last = [across, across + 1]
    for t in last:
        for k in range(3):
            y_copy(t, k, right, 0).wait_recv()
    vs = gather(last)
    for t in last:
        u_copy(t, right, 0).wait_recv()
    spread(last, vs)

    for e in range(4):
        tsend[0, e] = acc[e].astype(BF)
        tsend[1, e] = acc[12 + e].astype(BF)
    swaps = [(has_down, has_up, remote(tsend.at[0], trecv.at[0], t_sem.at[0], t_sem.at[1], down)),
             (has_up, has_down, remote(tsend.at[1], trecv.at[1], t_sem.at[2], t_sem.at[3], up))]
    for there, _, copy in swaps:
        when(there, copy.start)

    for w in range(2):
        t = 0
        for k in range(NBR):
            t = t + jnp.where(slot[0, k] == 2 * g + w, k, 0)
        t = jnp.minimum(t, NBR - 1)
        _, pos, s = picks(t)
        u = factor(t)
        us = split(u)
        for a in range(PAT):
            k = jnp.where(pos[1] == a, 1, jnp.where(pos[2] == a, 2, 0))
            self_ = (s == a).astype(F32)
            out_f[w, :, B * a:B * a + B] = u * self_ - mm(us, (yall[t, k, 0], yall[t, k, 1])) * (1.0 - self_)

    for there, back, copy in swaps:
        when(there, copy.wait_send)
        when(back, copy.wait_recv)
    for e in range(4):
        out_x[:, B * e:B * e + B] = acc[4 + e] + trecv[1, e].astype(F32)
        out_x[:, B * (4 + e):B * (4 + e) + B] = acc[8 + e] + trecv[0, e].astype(F32)
    for there, copy in sends:
        when(there, copy.wait_send)
    for copy in y_sends + u_sends:
        copy.wait_send()


def hand_on(factor, result, out_f, out_x):
    out_f[...] = factor[...]
    out_x[...] = result[...]


def solution(mesh):
    rows = mesh.shape["rows"]
    smem = pl.BlockSpec(memory_space=pltpu.SMEM)
    raw = pl.BlockSpec(memory_space=pltpu.HBM)
    whole = pl.BlockSpec(memory_space=pltpu.VMEM)

    def local(tile_factor, coupling, nbr_list, setup_slot, residual):
        columns = residual.shape[0]
        dma = pltpu.SemaphoreType.DMA
        factor, result = pl.pallas_call(
            functools.partial(kernel, rows),
            out_shape=(
                jax.ShapeDtypeStruct((2, B, PAT * B), F32),
                jax.ShapeDtypeStruct((columns, NBR * B), F32),
            ),
            in_specs=[smem, smem, raw, raw, raw],
            out_specs=(whole, whole),
            scratch_shapes=[
                pltpu.VMEM((10, 4, B, B), BF),
                pltpu.VMEM((NBR, 3, 2, B, B), BF),
                pltpu.VMEM((NBR, HALF + HALF // 2, B), F32),
                pltpu.VMEM((16, columns, B), F32),
                pltpu.VMEM((16, columns, B), F32),
                pltpu.VMEM((2, 4, columns, B), BF),
                pltpu.VMEM((2, 4, columns, B), BF),
                pltpu.VMEM((10, B, B), F32),
                dma((4,)), dma((8,)), dma((10, 4)), dma((10, 4)), dma((6, 3)), dma((NBR, 3)),
                dma((6,)), dma((NBR,)), dma((4,)), dma((4, 4)),
            ],
            compiler_params=pltpu.CompilerParams(
                collective_id=0, has_side_effects=True, vmem_limit_bytes=67043328
            ),
        )(nbr_list.T, setup_slot, tile_factor, coupling, residual)
        return pl.pallas_call(
            hand_on,
            out_shape=(jax.ShapeDtypeStruct(factor.shape, F32), jax.ShapeDtypeStruct(result.shape, F32)),
            in_specs=[whole, whole],
            out_specs=(whole, whole),
        )(factor, result)

    return jax.shard_map(
        local,
        mesh=mesh,
        in_specs=(
            P(("rows", "grp"), None, None),
            P(("rows", "grp"), None, None, None),
            P("rows", None),
            P("rows", None),
            P("grp", "rows"),
        ),
        out_specs=(P(("rows", "grp"), None, None), P("grp", "rows")),
        check_vma=False,
    )
```
